32 devices in a mesh: tile: 8 (over y, x, core), trac: 4 (over z).
Axes of the slice: x: 2, y: 2, z: 4, core: 2. Of those that a mesh axis runs over, the one named last changes fastest.
Arguments:
- tracers: float32 [128, 512, 128], P(None, ('tile', 'trac')), may hold values from -6 to 6
- winds: float32 [2, 512, 128], P(None, ('tile', 'trac')), may hold values from -4 to 4
- chem_linear: float32 [128, 128], replicated, may hold values from -0.5 to 0.5
- chem_loss: float32 [128], replicated, may hold values from 0.5 to 4
- chem_left: float32 [4, 128, 128], replicated, may hold values from -0.25 to 0.25
- chem_right: float32 [4, 128, 128], replicated, may hold values from -0.25 to 0.25
- active_cells: int32 [32], P(('tile', 'trac')), may hold values from 256 to 2048
Outputs:
- tracers_out: float32 [128, 512, 128], P(None, ('tile', 'trac'))
- winds_out: float32 [2, 512, 128], P(None, ('tile', 'trac'))
The draws below stay inside these ranges and needn't reach their ends.
Inputs may be any that keep to these rules, and one draw needn't show every extreme that they name: `active_cells`: active cells are the leading ones of the tile in row-major order.
All inputs are finite; a program needn't handle non-finite values.
Results may differ from the reference program's by a relative error of at most 0.0003.
Values sent between devices are 32-bit elements; how exact they have to be, the bound alone decides.
A program may use at most 64 MiB of HBM per device.

```python
import math
from functools import partial
import jax
import jax.numpy as jnp
from jax import lax

SPECIES = 128
W = 128
SUBS = 4
CHEM_STEPS = 3
PAIRS = 4
TILES = 32
ROWS = 512
CELLS = 2048


def with_ends(result, rng, smallest, largest):
    extent = result.shape
    spot = [jax.random.randint(jax.random.fold_in(rng, axis), (), 0, extent[axis]) for axis in range(len(extent))]
    result = result.at[tuple(spot)].set(smallest)
    longest = extent.index(max(extent))
    spot[longest] = (spot[longest] + 1) % extent[longest]
    return result.at[tuple(spot)].set(largest)


def levels(own_key, extent, shards, smallest, top_value):
    gain, own = 1.0, jax.random.fold_in(own_key, 6)
    for position, shards_of in shards:
        heights = jnp.exp(jax.random.uniform(jax.random.fold_in(own, position), (shards_of,), jnp.float32, smallest / len(shards), top_value / len(shards)))
        gain = gain * jnp.repeat(heights, extent[position] // shards_of).reshape([-1 if axis == position else 1 for axis in range(len(extent))])
    return gain


def scatter_about(key, dims, scale, reach, pieces=(), kind=jnp.bfloat16):
    entries = jax.random.normal(key, dims, jnp.float32) * scale
    if len(pieces) > 0:
        entries = levels(key, dims, pieces, -0.22, 0.18) * entries
    return jnp.clip(entries, min=-reach, max=reach).astype(kind)


def setup_inputs(seed: int = 0) -> dict:
    seeds = jax.random.split(jax.random.key(seed), 8)
    return {
        "tracers": scatter_about(seeds[0], (SPECIES, ROWS, W), 1.0, 6.0, ((1, 32),), jnp.float32),
        "winds": scatter_about(seeds[1], (2, ROWS, W), 1.0, 4.0, ((1, 32),), jnp.float32),
        "chem_linear": scatter_about(seeds[2], (SPECIES, SPECIES), SPECIES ** -0.5, 0.5, (), jnp.float32),
        "chem_loss": jnp.clip(jnp.exp(jax.random.uniform(seeds[3], (SPECIES,), jnp.float32, math.log(0.5), math.log(4.0))), 0.5, 4.0),
        "chem_left": scatter_about(seeds[4], (PAIRS, SPECIES, SPECIES), (4 * SPECIES) ** -0.5, 0.25, (), jnp.float32),
        "chem_right": scatter_about(seeds[5], (PAIRS, SPECIES, SPECIES), (4 * SPECIES) ** -0.5, 0.25, (), jnp.float32),
        "active_cells": with_ends(jax.random.randint(seeds[6], (TILES,), CELLS // 8, CELLS + 1), jax.random.fold_in(seeds[6], 1), CELLS // 8, CELLS).astype(jnp.int32),
    }


DT_WIND = 0.1
VISCOSITY = 0.2
DT_TRACER = 0.1
DT_CHEM = 0.1


def wrap_rows(field, width):
    return jnp.concatenate([field[:, field.shape[1] - width:, :], field, field[:, :width, :]], axis=1)


def tendency(extended):
    centre = extended[:, 1:-1, :]
    along = (jnp.roll(centre, -1, axis=2) - jnp.roll(centre, 1, axis=2)) * 0.5
    across = (extended[:, 2:, :] - extended[:, :-2, :]) * 0.5
    spread = jnp.roll(centre, -1, axis=2) + jnp.roll(centre, 1, axis=2) + extended[:, 2:, :] + extended[:, :-2, :] - 4.0 * centre
    return -(centre[0:1] * along + centre[1:2] * across) + VISCOSITY * spread


def wind_step(winds, rim):
    first = winds + DT_WIND * tendency(rim(winds))
    second = 0.75 * winds + 0.25 * (first + DT_WIND * tendency(rim(first)))
    return winds / 3.0 + 2.0 / 3.0 * (second + DT_WIND * tendency(rim(second)))


def advect(extended):
    tracer = extended[:-2]
    east = extended[-2, 1:-1, :]
    north = extended[-1]
    centre = tracer[:, 1:-1, :]
    flux = jnp.maximum(east, 0.0) * centre + jnp.minimum(jnp.roll(east, -1, axis=1), 0.0) * jnp.roll(centre, -1, axis=2)
    div_x = flux - jnp.roll(flux, 1, axis=2)
    upward = jnp.maximum(north[:-1], 0.0) * tracer[:, :-1, :] + jnp.minimum(north[1:], 0.0) * tracer[:, 1:, :]
    div_y = upward[:, 1:, :] - upward[:, :-1, :]
    moved = centre - DT_TRACER * (div_x + div_y)
    return jnp.concatenate([moved, extended[-2:, 1:-1, :]], axis=0)


def react(conc, active, linear, loss, both_factors):
    species = conc.shape[0]
    for step in range(CHEM_STEPS):
        rate = jnp.dot(linear, conc, precision=lax.Precision.HIGHEST, preferred_element_type=jnp.float32) - loss[:, None] * conc
        factors = jnp.dot(both_factors, conc, precision=lax.Precision.HIGHEST, preferred_element_type=jnp.float32)
        factors = factors.reshape(2, PAIRS, species, conc.shape[1])
        rate = rate + jnp.sum(factors[0] * factors[1], axis=0)
        conc = conc + DT_CHEM * (rate * active[None, :])
    return conc


def reference(tracers, winds, chem_linear, chem_loss, chem_left, chem_right, active_cells):
    rim = partial(wrap_rows, width=1)
    winds_new = wind_step(winds, rim)
    stretch = math.gcd(SPECIES, 8)
    grouped = tracers.reshape(SPECIES // stretch, stretch, ROWS, W)

    def carry_block(block):
        state = jnp.concatenate([block, winds_new], axis=0)
        for sub in range(SUBS):
            state = advect(rim(state))
        return state[:-2]

    moved = lax.map(carry_block, grouped).reshape(SPECIES, ROWS, W)
    tiled = moved.reshape(SPECIES, TILES, CELLS).transpose(1, 0, 2)
    both_factors = jnp.concatenate([chem_left, chem_right], axis=0).reshape(2 * PAIRS * SPECIES, SPECIES)

    def chem_tile(item):
        conc, count = item
        mask = (jnp.arange(CELLS, dtype=jnp.int32) < count).astype(jnp.float32)
        return react(conc, mask, chem_linear, chem_loss, both_factors)

    done = lax.map(chem_tile, (tiled, active_cells))
    return done.transpose(1, 0, 2).reshape(SPECIES, ROWS, W), winds_new
```

```python
import functools

import jax
import jax.numpy as jnp
from jax import lax
from jax.experimental import pallas as pl
from jax.experimental.pallas import tpu as pltpu
from jax.sharding import PartitionSpec as P

SUBS = 4
CHEM_STEPS = 3
WIND_STAGES = 3
PARTS = 4
LEAD = 2

DT_WIND = 0.1
VISCOSITY = 0.2
DT_TRACER = 0.1
DT_CHEM = 0.1

AXES = ("tile", "trac")
MESH = pl.DeviceIdType.MESH


def kernel(
    sizes,
    active,
    tracers,
    winds,
    linear,
    loss,
    left,
    right,
    done,
    wind_new,
    lev,
    wind,
    coef,
    lin_v,
    loss_v,
    fac_v,
    weights,
    row_sem,
    par_sem,
    wind_sem,
    send_sem,
    recv_sem,
    wsend_sem,
    wrecv_sem,
    count_ref,
    count_sem,
):
    tiles, tracs = sizes
    species, rows, width = tracers.shape
    pairs = left.shape[0]
    depth = SUBS
    reach = SUBS + WIND_STAGES
    wrows = wind.shape[1]
    base = (wrows - rows) // 2
    shift = base - depth
    devices = tiles * tracs
    me = lax.axis_index(AXES[0]) * tracs + lax.axis_index(AXES[1])
    up_flat = lax.rem(me + 1, devices)
    down_flat = lax.rem(me + devices - 1, devices)
    up = (up_flat // tracs, lax.rem(up_flat, tracs))
    down = (down_flat // tracs, lax.rem(down_flat, tracs))

    barrier = pltpu.get_barrier_semaphore()
    for neighbour in (up, down):
        pl.semaphore_signal(barrier, inc=1, device_id=neighbour, device_id_type=MESH)

    order = []
    for k in range(depth):
        order += [rows - 1 - k, k]
    order += list(range(depth, rows - depth))

    def row_copy(r):
        return pltpu.make_async_copy(tracers.at[:, r, :], lev.at[0, depth + r], row_sem.at[r])

    own_wind = pltpu.make_async_copy(winds, wind.at[:, base : base + rows, :], wind_sem)
    own_wind.start()
    for r in order:
        row_copy(r).start()
    params = [
        pltpu.make_async_copy(linear, lin_v, par_sem.at[0]),
        pltpu.make_async_copy(loss, loss_v, par_sem.at[1]),
        pltpu.make_async_copy(left, fac_v.at[0], par_sem.at[2]),
        pltpu.make_async_copy(right, fac_v.at[1], par_sem.at[3]),
    ]
    for copy in params:
        copy.start()
    count_copy = pltpu.make_async_copy(active, count_ref, count_sem)
    count_copy.start()

    def wind_send(side):
        first = rows - reach if side == 0 else 0
        there = base - reach if side == 0 else base + rows
        return pltpu.make_async_remote_copy(
            src_ref=winds.at[:, first : first + reach, :],
            dst_ref=wind.at[:, there : there + reach, :],
            send_sem=wsend_sem.at[side],
            recv_sem=wrecv_sem.at[side],
            device_id=up if side == 0 else down,
            device_id_type=MESH,
        )

    def halo_send(side, k):
        here = rows - 1 - k if side == 0 else k
        there = depth - 1 - k if side == 0 else depth + rows + k
        return pltpu.make_async_remote_copy(
            src_ref=tracers.at[:, here, :],
            dst_ref=lev.at[0, there],
            send_sem=send_sem.at[side, k],
            recv_sem=recv_sem.at[side, k],
            device_id=up if side == 0 else down,
            device_id_type=MESH,
        )

    pl.semaphore_wait(barrier, 2)
    place = lax.axis_index(AXES[1])
    last = tracs - 1

    @pl.when(jnp.logical_and(place > 0, place < last))
    def _():
        for side in range(2):
            wind_send(side).start()
        for k in range(depth):
            for side in range(2):
                halo_send(side, k).start()

    for end, near in ((0, 0), (last, 1)):

        @pl.when(place == end)
        def _(near=near):
            wind_send(1 - near).start()
            wind_send(near).start()
            for k in range(depth + LEAD):
                if k < depth:
                    halo_send(1 - near, k).start()
                if k >= LEAD:
                    halo_send(near, k - LEAD).start()

    for copy in params:
        copy.wait()
    diag = lax.broadcasted_iota(jnp.int32, (species, species), 0) == lax.broadcasted_iota(
        jnp.int32, (species, species), 1
    )

    block = species // PARTS
    height = (1 + 2 * pairs) * block

    def put(slot, value):
        high = value.astype(jnp.bfloat16)
        low = (value - high.astype(jnp.float32)).astype(jnp.bfloat16)
        for part in range(PARTS):
            lines = pl.ds((part * (1 + 2 * pairs) + slot) * block, block)
            own = slice(part * block, (part + 1) * block)
            weights[lines, :species] = high[own]
            weights[lines, species : 2 * species] = low[own]

    put(0, DT_CHEM * (lin_v[...] - jnp.where(diag, loss_v[...], 0.0)))
    for p in range(pairs):
        put(1 + p, DT_CHEM * fac_v[0, p])
        put(1 + pairs + p, fac_v[1, p])

    for r in range(rows):
        row_copy(r).wait()
    own_wind.wait()

    def update_winds(lines):
        raw = wind[:, lines]
        u0, v0 = raw[0], raw[1]
        held = u0.shape[0]

        def tendency(u, v):
            def of(f):
                east = pltpu.roll(f, width - 1, 1)
                west = pltpu.roll(f, 1, 1)
                north = pltpu.roll(f, held - 1, 0)
                south = pltpu.roll(f, 1, 0)
                along = (east - west) * 0.5
                across = (north - south) * 0.5
                spread = east + west + north + south - 4.0 * f
                return -(u * along + v * across) + VISCOSITY * spread

            return of(u), of(v)

        tu, tv = tendency(u0, v0)
        u1, v1 = u0 + DT_WIND * tu, v0 + DT_WIND * tv
        tu, tv = tendency(u1, v1)
        u2 = 0.75 * u0 + 0.25 * (u1 + DT_WIND * tu)
        v2 = 0.75 * v0 + 0.25 * (v1 + DT_WIND * tv)
        tu, tv = tendency(u2, v2)
        u3 = u0 / 3.0 + 2.0 / 3.0 * (u2 + DT_WIND * tu)
        v3 = v0 / 3.0 + 2.0 / 3.0 * (v2 + DT_WIND * tv)
        if held == wrows:
            wind_new[0] = u3[base : base + rows]
            wind_new[1] = v3[base : base + rows]
        coef[0, lines] = 1.0 - DT_TRACER * (jnp.abs(u3) + jnp.abs(v3))
        coef[1, lines] = pltpu.roll(DT_TRACER * jnp.maximum(u3, 0.0), 1, 1)
        coef[2, lines] = pltpu.roll(-DT_TRACER * jnp.minimum(u3, 0.0), width - 1, 1)
        coef[3, lines] = pltpu.roll(DT_TRACER * jnp.maximum(v3, 0.0), 1, 0)
        coef[4, lines] = pltpu.roll(-DT_TRACER * jnp.minimum(v3, 0.0), held - 1, 0)

    def line(i):
        return pl.ds(i + shift, 1)

    def spread(level, i):
        q = lev[level - 1, i]
        moved = coef[0, line(i), :] * q
        moved += coef[1, line(i), :] * pltpu.roll(q, 1, 1)
        moved += coef[2, line(i), :] * pltpu.roll(q, width - 1, 1)
        return moved

    def advance(level, i):
        moved = spread(level, i)
        moved += coef[3, line(i), :] * lev[level - 1, i - 1]
        moved += coef[4, line(i), :] * lev[level - 1, i + 1]
        lev[level, i] = moved

    def sweep(spans):
        for level, first, last in spans:
            for i in range(first, last):
                advance(level, i)
                yield

    count_copy.wait()
    count = count_ref[0]
    lane = lax.broadcasted_iota(jnp.int32, (1, width), 1)

    def react(couples, values=None):
        concs, masks = [], []
        for n, (first, second) in enumerate(couples):
            pair = (lev[depth, first], lev[depth, second]) if values is None else values[n]
            concs.append(jnp.concatenate(pair, axis=1))
            cell = jnp.concatenate(
                [(first - depth) * width + lane, (second - depth) * width + lane], axis=1
            )
            masks.append(jnp.where(cell < count, 1.0, 0.0))
        for step in range(CHEM_STEPS):
            for j, mask in enumerate(masks):
                conc = concs[j]
                high = conc.astype(jnp.bfloat16)
                low = (conc - high.astype(jnp.float32)).astype(jnp.bfloat16)
                high = jnp.concatenate([high, high], axis=0)
                low = jnp.concatenate([low, low], axis=0)
                blocks = []
                for part in range(PARTS):
                    lhs = weights[part * height : (part + 1) * height]
                    terms = jnp.dot(lhs, high, preferred_element_type=jnp.float32) + jnp.dot(
                        lhs, low, preferred_element_type=jnp.float32
                    )
                    rate = terms[:block]
                    for p in range(pairs):
                        one = (1 + p) * block
                        two = (1 + pairs + p) * block
                        rate += terms[one : one + block] * terms[two : two + block]
                    blocks.append(conc[part * block : (part + 1) * block] + rate * mask)
                    yield
                concs[j] = jnp.concatenate(blocks, axis=0)
        for (first, second), conc in zip(couples, concs):
            done[first - depth] = conc[:, :width]
            done[second - depth] = conc[:, width:]

    def weave(main, side=(), pace=1):
        side = iter(side)
        for _ in main:
            for _ in range(pace):
                next(side, None)
        for _ in side:
            pass

    update_winds(slice(base, base + rows))
    low, high = depth, depth + rows
    levels = range(1, depth + 1)
    inner = [(n, low + WIND_STAGES + n, high - WIND_STAGES - n) for n in levels]
    rims = []
    for n in levels:
        rims += [(n, low + n, low + WIND_STAGES + n), (n, high - WIND_STAGES - n, high - n)]
    weave(sweep(inner))

    for side in range(2):
        wind_send(side).wait()
    update_winds(slice(0, wrows))

    def ready(k):
        for n in levels:
            for i, near in ((low - 1 - k + n, 1), (high + k - n, -1)):
                lev[n, i] = spread(n, i) + coef[3 if near < 0 else 4, line(i), :] * lev[n - 1, i + near]
                yield

    def arrive(k):
        for side in range(2):
            halo_send(side, k).wait()
        south, north = lev[0, low - 1 - k], lev[0, high + k]
        for n in levels:
            i, j = low - 1 - k + n, high + k - n
            south = lev[n, i] + coef[3, line(i), :] * south
            north = lev[n, j] + coef[4, line(j), :] * north
            lev[n, i] = south
            lev[n, j] = north
        return south, north

    couples = [(low + depth + i, high - depth - 1 - i) for i in reversed(range(-depth, WIND_STAGES + 1))]
    first = couples[:1]
    assert 2 * WIND_STAGES + 2 == rows - 2 * depth
    weave(react(first), sweep(rims), -(-2 * WIND_STAGES * depth // (PARTS * CHEM_STEPS)))
    inside = couples[1 : 1 + WIND_STAGES]
    weave(react(inside), ready(0))
    for k in range(depth):
        values = arrive(k)
        weave(react([couples[1 + WIND_STAGES + k]], [values]), ready(k + 1) if k + 1 < depth else (), -(-2 * depth // (PARTS * CHEM_STEPS)))


def finish(done, wind_new, tracers_out, winds_out, out_sem, wind_sem):
    copies = [pltpu.make_async_copy(wind_new, winds_out, wind_sem)]
    for r in range(done.shape[0]):
        copies.append(pltpu.make_async_copy(done.at[r], tracers_out.at[:, r, :], out_sem.at[r]))
    for copy in copies:
        copy.start()
    for copy in copies:
        copy.wait()


def on_device(sizes, tracers, winds, linear, loss, left, right, active):
    species, rows, width = tracers.shape
    pairs = left.shape[0]
    held = rows + 2 * SUBS
    wrows = rows + 2 * (-(-(SUBS + WIND_STAGES) // 8) * 8)
    f32 = jnp.float32
    dma = pltpu.SemaphoreType.DMA
    anywhere = pl.BlockSpec(memory_space=pl.ANY)
    vmem = pl.BlockSpec(memory_space=pltpu.VMEM)
    done, wind_new = pl.pallas_call(
        functools.partial(kernel, sizes),
        out_shape=(
            pltpu.VMEM((rows, species, width), f32),
            pltpu.VMEM(winds.shape, f32),
        ),
        in_specs=[anywhere] * 7,
        out_specs=(vmem, vmem),
        scratch_shapes=[
            pltpu.VMEM((SUBS + 1, held, species, width), f32),
            pltpu.VMEM((2, wrows, width), f32),
            pltpu.VMEM((5, wrows, width), f32),
            pltpu.VMEM(linear.shape, f32),
            pltpu.VMEM((1, species), f32),
            pltpu.VMEM((2,) + left.shape, f32),
            pltpu.VMEM(((1 + 2 * pairs) * species, 2 * species), jnp.bfloat16),
            dma((rows,)),
            dma((4,)),
            dma,
            dma((2, SUBS)),
            dma((2, SUBS)),
            dma((2,)),
            dma((2,)),
            pltpu.SMEM(active.shape, active.dtype),
            dma,
        ],
        compiler_params=pltpu.CompilerParams(collective_id=0, has_side_effects=True),
    )(active, tracers, winds, linear, loss.reshape(1, species), left, right)
    return pl.pallas_call(
        finish,
        out_shape=(
            jax.ShapeDtypeStruct(tracers.shape, f32),
            jax.ShapeDtypeStruct(winds.shape, f32),
        ),
        in_specs=[vmem, vmem],
        out_specs=(anywhere, anywhere),
        scratch_shapes=[dma((rows,)), dma],
    )(
        pltpu.with_memory_space_constraint(done, pltpu.VMEM),
        pltpu.with_memory_space_constraint(wind_new, pltpu.VMEM),
    )


def solution(mesh):
    sizes = tuple(mesh.shape[axis] for axis in AXES)
    banded = P(None, AXES, None)
    return jax.shard_map(
        functools.partial(on_device, sizes),
        mesh=mesh,
        in_specs=(banded, banded, P(), P(), P(), P(), P(AXES)),
        out_specs=(banded, banded),
        check_vma=False,
    )
```

```python
import functools

import jax
import jax.numpy as jnp
from jax import lax
from jax.experimental import pallas as pl
from jax.experimental.pallas import tpu as pltpu
from jax.sharding import PartitionSpec as P

SUBS = 4
CHEM_STEPS = 3
WIND_STAGES = 3
PARTS = 8
LEAD = (1, 1)
EARLY = 2
MIDDLE = 4
LATE = 1

DT_WIND = 0.1
VISCOSITY = 0.2
DT_TRACER = 0.1
DT_CHEM = 0.1

AXES = ("tile", "trac")
MESH = pl.DeviceIdType.MESH


def kernel(
    sizes,
    active,
    tracers,
    winds,
    linear,
    loss,
    left,
    right,
    done,
    wind_new,
    lev,
    wind,
    coef,
    lin_v,
    loss_v,
    fac_v,
    weights,
    row_sem,
    par_sem,
    wind_sem,
    send_sem,
    recv_sem,
    wsend_sem,
    wrecv_sem,
    count_ref,
    count_sem,
    joined,
):
    tiles, tracs = sizes
    species, rows, width = tracers.shape
    pairs = left.shape[0]
    depth = SUBS
    reach = SUBS + WIND_STAGES
    wrows = wind.shape[1]
    base = (wrows - rows) // 2
    shift = base - depth
    devices = tiles * tracs
    me = lax.axis_index(AXES[0]) * tracs + lax.axis_index(AXES[1])
    up_flat = lax.rem(me + 1, devices)
    down_flat = lax.rem(me + devices - 1, devices)
    up = (up_flat // tracs, lax.rem(up_flat, tracs))
    down = (down_flat // tracs, lax.rem(down_flat, tracs))

    place = lax.axis_index(AXES[1])
    last = tracs - 1

    def tell(semaphore, neighbour):
        pl.semaphore_signal(semaphore, inc=1, device_id=neighbour, device_id_type=MESH)

    barrier = pltpu.get_barrier_semaphore()

    @pl.when(place < last)
    def _():
        tell(barrier, up)

    @pl.when(place < 2)
    def _():
        tell(barrier, down)


    order = []
    for k in range(depth):
        order += [rows - 1 - k, k]
    order += list(range(depth, rows - depth))

    def row_copy(r):
        return pltpu.make_async_copy(tracers.at[:, r, :], lev.at[0, depth + r], row_sem.at[r])

    own_wind = pltpu.make_async_copy(winds, wind.at[:, base : base + rows, :], wind_sem)
    own_wind.start()
    for r in order:
        row_copy(r).start()
    params = [
        pltpu.make_async_copy(linear, lin_v, par_sem.at[0]),
        pltpu.make_async_copy(loss, loss_v, par_sem.at[1]),
        pltpu.make_async_copy(left, fac_v.at[0], par_sem.at[2]),
        pltpu.make_async_copy(right, fac_v.at[1], par_sem.at[3]),
    ]
    for copy in params:
        copy.start()
    count_copy = pltpu.make_async_copy(active, count_ref, count_sem)
    count_copy.start()

    def wind_send(side):
        first = rows - reach if side == 0 else 0
        there = base - reach if side == 0 else base + rows
        return pltpu.make_async_remote_copy(
            src_ref=winds.at[:, first : first + reach, :],
            dst_ref=wind.at[:, there : there + reach, :],
            send_sem=wsend_sem.at[side],
            recv_sem=wrecv_sem.at[side],
            device_id=up if side == 0 else down,
            device_id_type=MESH,
        )

    def halo_send(side, k):
        here = rows - 1 - k if side == 0 else k
        there = depth - 1 - k if side == 0 else depth + rows + k
        return pltpu.make_async_remote_copy(
            src_ref=tracers.at[:, here, :],
            dst_ref=lev.at[0, there],
            send_sem=send_sem.at[side, k],
            recv_sem=recv_sem.at[side, k],
            device_id=up if side == 0 else down,
            device_id_type=MESH,
        )

    pl.semaphore_wait(barrier, jnp.where(place == last, 2, 1))

    @pl.when(place > 1)
    def _():
        tell(joined, down)

    @pl.when(place == last)
    def _():
        tell(joined, up)

    def send(side):
        wind_send(side).start()
        for k in range(MIDDLE):
            halo_send(side, k).start()

    def late(at):
        if at != LATE:
            return

        @pl.when(jnp.logical_and(place > 0, place < last))
        def _():
            for k in range(MIDDLE, depth):
                for side in range(2):
                    halo_send(side, k).start()

    def both(near, lead, early):
        turns = [(2 * k + 1, near, k) for k in range(early, depth)]
        turns += [(2 * (k - lead), 1 - near, k) for k in range(depth)]
        for _, side, k in sorted(turns):
            halo_send(side, k).start()

    @pl.when(place == 0)
    def _():
        wind_send(0).start()
        for k in range(EARLY):
            halo_send(0, k).start()

    @pl.when(jnp.logical_and(place > 0, place < last))
    def _():
        send(1)
        pl.semaphore_wait(joined, 1)
        send(0)

    @pl.when(place == last)
    def _():
        wind_send(0).start()
        wind_send(1).start()
        both(1, LEAD[1], 0)

    for copy in params:
        copy.wait()
    diag = lax.broadcasted_iota(jnp.int32, (species, species), 0) == lax.broadcasted_iota(
        jnp.int32, (species, species), 1
    )

    block = species // PARTS
    height = (1 + 2 * pairs) * block

    def put(slot, value):
        high = value.astype(jnp.bfloat16)
        low = (value - high.astype(jnp.float32)).astype(jnp.bfloat16)
        for part in range(PARTS):
            lines = pl.ds((part * (1 + 2 * pairs) + slot) * block, block)
            own = slice(part * block, (part + 1) * block)
            weights[lines, :species] = high[own]
            weights[lines, species : 2 * species] = low[own]

    put(0, DT_CHEM * (lin_v[...] - jnp.where(diag, loss_v[...], 0.0)))
    for p in range(pairs):
        put(1 + p, DT_CHEM * fac_v[0, p])
        put(1 + pairs + p, fac_v[1, p])

    for r in range(rows):
        row_copy(r).wait()
    own_wind.wait()

    def update_winds(lines):
        raw = wind[:, lines]
        u0, v0 = raw[0], raw[1]
        held = u0.shape[0]

        def tendency(u, v):
            def of(f):
                east = pltpu.roll(f, width - 1, 1)
                west = pltpu.roll(f, 1, 1)
                north = pltpu.roll(f, held - 1, 0)
                south = pltpu.roll(f, 1, 0)
                along = (east - west) * 0.5
                across = (north - south) * 0.5
                spread = east + west + north + south - 4.0 * f
                return -(u * along + v * across) + VISCOSITY * spread

            return of(u), of(v)

        tu, tv = tendency(u0, v0)
        u1, v1 = u0 + DT_WIND * tu, v0 + DT_WIND * tv
        tu, tv = tendency(u1, v1)
        u2 = 0.75 * u0 + 0.25 * (u1 + DT_WIND * tu)
        v2 = 0.75 * v0 + 0.25 * (v1 + DT_WIND * tv)
        tu, tv = tendency(u2, v2)
        u3 = u0 / 3.0 + 2.0 / 3.0 * (u2 + DT_WIND * tu)
        v3 = v0 / 3.0 + 2.0 / 3.0 * (v2 + DT_WIND * tv)
        if held == wrows:
            wind_new[0] = u3[base : base + rows]
            wind_new[1] = v3[base : base + rows]
        coef[0, lines] = 1.0 - DT_TRACER * (jnp.abs(u3) + jnp.abs(v3))
        coef[1, lines] = pltpu.roll(DT_TRACER * jnp.maximum(u3, 0.0), 1, 1)
        coef[2, lines] = pltpu.roll(-DT_TRACER * jnp.minimum(u3, 0.0), width - 1, 1)
        coef[3, lines] = pltpu.roll(DT_TRACER * jnp.maximum(v3, 0.0), 1, 0)
        coef[4, lines] = pltpu.roll(-DT_TRACER * jnp.minimum(v3, 0.0), held - 1, 0)

    def line(i):
        return pl.ds(i + shift, 1)

    def spread(level, i):
        q = lev[level - 1, i]
        moved = coef[0, line(i), :] * q
        moved += coef[1, line(i), :] * pltpu.roll(q, 1, 1)
        moved += coef[2, line(i), :] * pltpu.roll(q, width - 1, 1)
        return moved

    def advance(level, i):
        moved = spread(level, i)
        moved += coef[3, line(i), :] * lev[level - 1, i - 1]
        moved += coef[4, line(i), :] * lev[level - 1, i + 1]
        lev[level, i] = moved

    def sweep(spans):
        for level, first, last in spans:
            for i in range(first, last):
                advance(level, i)
                yield

    count_copy.wait()
    count = count_ref[0]
    lane = lax.broadcasted_iota(jnp.int32, (1, width), 1)

    def react(couples, values=None):
        concs, masks = [], []
        for n, (first, second) in enumerate(couples):
            pair = (lev[depth, first], lev[depth, second]) if values is None else values[n]
            concs.append(jnp.concatenate(pair, axis=1))
            cell = jnp.concatenate(
                [(first - depth) * width + lane, (second - depth) * width + lane], axis=1
            )
            masks.append(jnp.where(cell < count, 1.0, 0.0))
        for step in range(CHEM_STEPS):
            for j, mask in enumerate(masks):
                conc = concs[j]
                high = conc.astype(jnp.bfloat16)
                low = (conc - high.astype(jnp.float32)).astype(jnp.bfloat16)
                high = jnp.concatenate([high, high], axis=0)
                low = jnp.concatenate([low, low], axis=0)
                blocks = []
                for part in range(PARTS):
                    lhs = weights[part * height : (part + 1) * height]
                    terms = jnp.dot(lhs, high, preferred_element_type=jnp.float32) + jnp.dot(
                        lhs, low, preferred_element_type=jnp.float32
                    )
                    rate = terms[:block]
                    for p in range(pairs):
                        one = (1 + p) * block
                        two = (1 + pairs + p) * block
                        rate += terms[one : one + block] * terms[two : two + block]
                    blocks.append(conc[part * block : (part + 1) * block] + rate * mask)
                    yield
                concs[j] = jnp.concatenate(blocks, axis=0)
        for (first, second), conc in zip(couples, concs):
            done[first - depth] = conc[:, :width]
            done[second - depth] = conc[:, width:]

    def weave(main, side=(), pace=1):
        side = iter(side)
        for _ in main:
            for _ in range(pace):
                next(side, None)
        for _ in side:
            pass

    update_winds(slice(base, base + rows))
    low, high = depth, depth + rows
    levels = range(1, depth + 1)
    inner = [(n, low + WIND_STAGES + n, high - WIND_STAGES - n) for n in levels]
    couples = [(low + depth + i, high - depth - 1 - i) for i in reversed(range(-depth, WIND_STAGES + 1))]
    assert 2 * WIND_STAGES + 2 == rows - 2 * depth
    weave(sweep(inner))

    @pl.when(place == 0)
    def _():
        pl.semaphore_wait(joined, 1)
        wind_send(1).start()
        both(0, LEAD[0], EARLY)

    weave(react(couples[:1]))
    for side in range(2):
        wind_send(side).wait_recv()
    update_winds(slice(0, wrows))

    def ready(k):
        for n in levels:
            for i, near in ((low - 1 - k + n, 1), (high + k - n, -1)):
                lev[n, i] = spread(n, i) + coef[3 if near < 0 else 4, line(i), :] * lev[n - 1, i + near]
                yield

    def arrive(k):
        for side in range(2):
            halo_send(side, k).wait_recv()
        south, north = lev[0, low - 1 - k], lev[0, high + k]
        for n in levels:
            i, j = low - 1 - k + n, high + k - n
            south = lev[n, i] + coef[3, line(i), :] * south
            north = lev[n, j] + coef[4, line(j), :] * north
            lev[n, i] = south
            lev[n, j] = north
        return south, north

    def rim(d):
        for n in levels:
            for i in (low + WIND_STAGES + n - 1 - d, high - WIND_STAGES - n + d):
                advance(n, i)
                yield

    def chain(*parts):
        for part in parts:
            yield from part

    late(0)
    weave(rim(0))
    weave(react(couples[1:2]), chain(rim(1), rim(2)), 2)
    late(1)
    weave(react(couples[2 : 1 + WIND_STAGES]), ready(0))
    late(2)
    for k in range(depth):
        values = arrive(k)
        weave(react([couples[1 + WIND_STAGES + k]], [values]), ready(k + 1) if k + 1 < depth else (), -(-2 * depth // (PARTS * CHEM_STEPS)))
    for side in range(2):
        wind_send(side).wait_send()
        for k in range(depth):
            halo_send(side, k).wait_send()


def finish(done, wind_new, tracers_out, winds_out, out_sem, wind_sem):
    copies = [pltpu.make_async_copy(wind_new, winds_out, wind_sem)]
    for r in range(done.shape[0]):
        copies.append(pltpu.make_async_copy(done.at[r], tracers_out.at[:, r, :], out_sem.at[r]))
    for copy in copies:
        copy.start()
    for copy in copies:
        copy.wait()


def on_device(sizes, tracers, winds, linear, loss, left, right, active):
    species, rows, width = tracers.shape
    pairs = left.shape[0]
    held = rows + 2 * SUBS
    wrows = rows + 2 * (-(-(SUBS + WIND_STAGES) // 8) * 8)
    f32 = jnp.float32
    dma = pltpu.SemaphoreType.DMA
    anywhere = pl.BlockSpec(memory_space=pl.ANY)
    vmem = pl.BlockSpec(memory_space=pltpu.VMEM)
    done, wind_new = pl.pallas_call(
        functools.partial(kernel, sizes),
        out_shape=(
            pltpu.VMEM((rows, species, width), f32),
            pltpu.VMEM(winds.shape, f32),
        ),
        in_specs=[anywhere] * 7,
        out_specs=(vmem, vmem),
        scratch_shapes=[
            pltpu.VMEM((SUBS + 1, held, species, width), f32),
            pltpu.VMEM((2, wrows, width), f32),
            pltpu.VMEM((5, wrows, width), f32),
            pltpu.VMEM(linear.shape, f32),
            pltpu.VMEM((1, species), f32),
            pltpu.VMEM((2,) + left.shape, f32),
            pltpu.VMEM(((1 + 2 * pairs) * species, 2 * species), jnp.bfloat16),
            dma((rows,)),
            dma((4,)),
            dma,
            dma((2, SUBS)),
            dma((2, SUBS)),
            dma((2,)),
            dma((2,)),
            pltpu.SMEM(active.shape, active.dtype),
            dma,
            pltpu.SemaphoreType.REGULAR,
        ],
        compiler_params=pltpu.CompilerParams(collective_id=0, has_side_effects=True),
    )(active, tracers, winds, linear, loss.reshape(1, species), left, right)
    return pl.pallas_call(
        finish,
        out_shape=(
            jax.ShapeDtypeStruct(tracers.shape, f32),
            jax.ShapeDtypeStruct(winds.shape, f32),
        ),
        in_specs=[vmem, vmem],
        out_specs=(anywhere, anywhere),
        scratch_shapes=[dma((rows,)), dma],
    )(
        pltpu.with_memory_space_constraint(done, pltpu.VMEM),
        pltpu.with_memory_space_constraint(wind_new, pltpu.VMEM),
    )


def solution(mesh):
    sizes = tuple(mesh.shape[axis] for axis in AXES)
    banded = P(None, AXES, None)
    return jax.shard_map(
        functools.partial(on_device, sizes),
        mesh=mesh,
        in_specs=(banded, banded, P(), P(), P(), P(), P(AXES)),
        out_specs=(banded, banded),
        check_vma=False,
    )
```

```python
import functools

import jax
import jax.numpy as jnp
from jax import lax
from jax.experimental import pallas as pl
from jax.experimental.pallas import tpu as pltpu
from jax.sharding import PartitionSpec as P

SUBS = 4
CHEM_STEPS = 3
WIND_STAGES = 3
PARTS = 4
PIECES = 2
LEAD = (2, 2)
EARLY = 2
MIDDLE = 4
LATE = 0

DT_WIND = 0.1
VISCOSITY = 0.2
DT_TRACER = 0.1
DT_CHEM = 0.1

AXES = ("tile", "trac")
MESH = pl.DeviceIdType.MESH


def chemistry(weights, concs, masks, store=None):
    species = concs[0].shape[0]
    block = species // PARTS
    height = weights.shape[0] // PARTS
    pairs = (height // block - 1) // 2
    for step in range(CHEM_STEPS):
        for j, mask in enumerate(masks):
            conc = concs[j]
            high = conc.astype(jnp.bfloat16)
            low = (conc - high.astype(jnp.float32)).astype(jnp.bfloat16)
            high = jnp.concatenate([high, high], axis=0)
            low = jnp.concatenate([low, low], axis=0)
            blocks = []
            for part in range(PARTS):
                lhs = weights[part * height : (part + 1) * height]
                terms = jnp.dot(lhs, high, preferred_element_type=jnp.float32) + jnp.dot(
                    lhs, low, preferred_element_type=jnp.float32
                )
                rate = terms[:block]
                for p in range(pairs):
                    one = (1 + p) * block
                    two = (1 + pairs + p) * block
                    rate += terms[one : one + block] * terms[two : two + block]
                blocks.append(conc[part * block : (part + 1) * block] + rate * mask)
                if store is not None and step == CHEM_STEPS - 1:
                    store(part, blocks[-1])
                yield
            concs[j] = jnp.concatenate(blocks, axis=0)


def kernel(
    sizes,
    active,
    tracers,
    winds,
    linear,
    loss,
    left,
    right,
    done,
    wind_new,
    weights,
    mask_out,
    lev,
    wind,
    coef,
    lin_v,
    loss_v,
    fac_v,
    row_sem,
    par_sem,
    wind_sem,
    send_sem,
    recv_sem,
    wsend_sem,
    wrecv_sem,
    count_ref,
    count_sem,
    joined,
):
    tiles, tracs = sizes
    species, rows, width = tracers.shape
    pairs = left.shape[0]
    depth = SUBS
    reach = SUBS + WIND_STAGES
    wrows = wind.shape[1]
    base = (wrows - rows) // 2
    shift = base - depth
    devices = tiles * tracs
    me = lax.axis_index(AXES[0]) * tracs + lax.axis_index(AXES[1])
    up_flat = lax.rem(me + 1, devices)
    down_flat = lax.rem(me + devices - 1, devices)
    up = (up_flat // tracs, lax.rem(up_flat, tracs))
    down = (down_flat // tracs, lax.rem(down_flat, tracs))

    place = lax.axis_index(AXES[1])
    last = tracs - 1

    def tell(semaphore, neighbour):
        pl.semaphore_signal(semaphore, inc=1, device_id=neighbour, device_id_type=MESH)

    barrier = pltpu.get_barrier_semaphore()

    @pl.when(place < last)
    def _():
        tell(barrier, up)

    @pl.when(place < 2)
    def _():
        tell(barrier, down)


    order = []
    for k in range(depth):
        order += [rows - 1 - k, k]
    order += list(range(depth, rows - depth))

    def row_copy(r):
        return pltpu.make_async_copy(tracers.at[:, r, :], lev.at[0, depth + r], row_sem.at[r])

    own_wind = pltpu.make_async_copy(winds, wind.at[:, base : base + rows, :], wind_sem)
    own_wind.start()
    for r in order:
        row_copy(r).start()
    params = [
        pltpu.make_async_copy(linear, lin_v, par_sem.at[0]),
        pltpu.make_async_copy(loss, loss_v, par_sem.at[1]),
        pltpu.make_async_copy(left, fac_v.at[0], par_sem.at[2]),
        pltpu.make_async_copy(right, fac_v.at[1], par_sem.at[3]),
    ]
    for copy in params:
        copy.start()
    count_copy = pltpu.make_async_copy(active, count_ref, count_sem)
    count_copy.start()

    def wind_send(side):
        first = rows - reach if side == 0 else 0
        there = base - reach if side == 0 else base + rows
        return pltpu.make_async_remote_copy(
            src_ref=winds.at[:, first : first + reach, :],
            dst_ref=wind.at[:, there : there + reach, :],
            send_sem=wsend_sem.at[side],
            recv_sem=wrecv_sem.at[side],
            device_id=up if side == 0 else down,
            device_id_type=MESH,
        )

    def halo_send(side, k):
        here = rows - 1 - k if side == 0 else k
        there = depth - 1 - k if side == 0 else depth + rows + k
        return pltpu.make_async_remote_copy(
            src_ref=tracers.at[:, here, :],
            dst_ref=lev.at[0, there],
            send_sem=send_sem.at[side, k],
            recv_sem=recv_sem.at[side, k],
            device_id=up if side == 0 else down,
            device_id_type=MESH,
        )

    pl.semaphore_wait(barrier, jnp.where(place == last, 2, 1))

    @pl.when(place > 1)
    def _():
        tell(joined, down)

    @pl.when(place == last)
    def _():
        tell(joined, up)

    def send(side):
        wind_send(side).start()
        for k in range(MIDDLE):
            halo_send(side, k).start()

    def late(at):
        if at != LATE:
            return

        @pl.when(jnp.logical_and(place > 0, place < last))
        def _():
            for k in range(MIDDLE, depth):
                for side in range(2):
                    halo_send(side, k).start()

    def both(near, lead, early):
        turns = [(2 * k + 1, near, k) for k in range(early, depth)]
        turns += [(2 * (k - lead), 1 - near, k) for k in range(depth)]
        for _, side, k in sorted(turns):
            halo_send(side, k).start()

    @pl.when(place == 0)
    def _():
        wind_send(0).start()
        for k in range(EARLY):
            halo_send(0, k).start()

    @pl.when(jnp.logical_and(place > 0, place < last))
    def _():
        send(1)
        pl.semaphore_wait(joined, 1)
        send(0)

    @pl.when(place == last)
    def _():
        wind_send(0).start()
        wind_send(1).start()
        both(1, LEAD[1], 0)

    for copy in params:
        copy.wait()
    diag = lax.broadcasted_iota(jnp.int32, (species, species), 0) == lax.broadcasted_iota(
        jnp.int32, (species, species), 1
    )

    block = species // PARTS
    height = (1 + 2 * pairs) * block

    def put(slot, value):
        high = value.astype(jnp.bfloat16)
        low = (value - high.astype(jnp.float32)).astype(jnp.bfloat16)
        for part in range(PARTS):
            lines = pl.ds((part * (1 + 2 * pairs) + slot) * block, block)
            own = slice(part * block, (part + 1) * block)
            weights[lines, :species] = high[own]
            weights[lines, species : 2 * species] = low[own]

    put(0, DT_CHEM * (lin_v[...] - jnp.where(diag, loss_v[...], 0.0)))
    for p in range(pairs):
        put(1 + p, DT_CHEM * fac_v[0, p])
        put(1 + pairs + p, fac_v[1, p])

    for r in range(rows):
        row_copy(r).wait()
    own_wind.wait()

    def update_winds(lines):
        raw = wind[:, lines]
        u0, v0 = raw[0], raw[1]
        held = u0.shape[0]

        def tendency(u, v):
            def of(f):
                east = pltpu.roll(f, width - 1, 1)
                west = pltpu.roll(f, 1, 1)
                north = pltpu.roll(f, held - 1, 0)
                south = pltpu.roll(f, 1, 0)
                along = (east - west) * 0.5
                across = (north - south) * 0.5
                spread = east + west + north + south - 4.0 * f
                return -(u * along + v * across) + VISCOSITY * spread

            return of(u), of(v)

        tu, tv = tendency(u0, v0)
        u1, v1 = u0 + DT_WIND * tu, v0 + DT_WIND * tv
        tu, tv = tendency(u1, v1)
        u2 = 0.75 * u0 + 0.25 * (u1 + DT_WIND * tu)
        v2 = 0.75 * v0 + 0.25 * (v1 + DT_WIND * tv)
        tu, tv = tendency(u2, v2)
        u3 = u0 / 3.0 + 2.0 / 3.0 * (u2 + DT_WIND * tu)
        v3 = v0 / 3.0 + 2.0 / 3.0 * (v2 + DT_WIND * tv)
        if held == wrows:
            wind_new[0] = u3[base : base + rows]
            wind_new[1] = v3[base : base + rows]
        coef[0, lines] = 1.0 - DT_TRACER * (jnp.abs(u3) + jnp.abs(v3))
        coef[1, lines] = pltpu.roll(DT_TRACER * jnp.maximum(u3, 0.0), 1, 1)
        coef[2, lines] = pltpu.roll(-DT_TRACER * jnp.minimum(u3, 0.0), width - 1, 1)
        coef[3, lines] = pltpu.roll(DT_TRACER * jnp.maximum(v3, 0.0), 1, 0)
        coef[4, lines] = pltpu.roll(-DT_TRACER * jnp.minimum(v3, 0.0), held - 1, 0)

    def line(i):
        return pl.ds(i + shift, 1)

    def spread(level, i):
        q = lev[level - 1, i]
        moved = coef[0, line(i), :] * q
        moved += coef[1, line(i), :] * pltpu.roll(q, 1, 1)
        moved += coef[2, line(i), :] * pltpu.roll(q, width - 1, 1)
        return moved

    def advance(level, i):
        moved = spread(level, i)
        moved += coef[3, line(i), :] * lev[level - 1, i - 1]
        moved += coef[4, line(i), :] * lev[level - 1, i + 1]
        lev[level, i] = moved

    def sweep(spans):
        for level, first, last in spans:
            for i in range(first, last):
                advance(level, i)
                yield

    count_copy.wait()
    count = count_ref[0]
    lane = lax.broadcasted_iota(jnp.int32, (1, width), 1)

    def mask_of(*pair):
        cell = jnp.concatenate([(i - depth) * width + lane for i in pair], axis=1)
        return jnp.where(cell < count, 1.0, 0.0)

    def react(couples, values=None):
        concs, masks = [], []
        for n, (first, second) in enumerate(couples):
            pair = (lev[depth, first], lev[depth, second]) if values is None else values[n]
            concs.append(jnp.concatenate(pair, axis=1))
            masks.append(mask_of(first, second))
        yield from chemistry(weights, concs, masks)
        for (first, second), conc in zip(couples, concs):
            done[first - depth] = conc[:, :width]
            done[second - depth] = conc[:, width:]

    def weave(main, side=(), pace=1):
        side = iter(side)
        for _ in main:
            for _ in range(pace):
                next(side, None)
        for _ in side:
            pass

    update_winds(slice(base, base + rows))
    low, high = depth, depth + rows
    levels = range(1, depth + 1)
    inner = [(n, low + WIND_STAGES + n, high - WIND_STAGES - n) for n in levels]
    couples = [(low + depth + i, high - depth - 1 - i) for i in reversed(range(-depth, WIND_STAGES + 1))]
    assert 2 * WIND_STAGES + 2 == rows - 2 * depth
    weave(sweep(inner))

    @pl.when(place == 0)
    def _():
        pl.semaphore_wait(joined, 1)
        wind_send(1).start()
        both(0, LEAD[0], EARLY)

    weave(react(couples[:1]))
    for side in range(2):
        wind_send(side).wait_recv()
    update_winds(slice(0, wrows))

    def ready(k):
        for n in levels:
            for i, near in ((low - 1 - k + n, 1), (high + k - n, -1)):
                lev[n, i] = spread(n, i) + coef[3 if near < 0 else 4, line(i), :] * lev[n - 1, i + near]
                yield

    def arrive(k):
        for side in range(2):
            halo_send(side, k).wait_recv()
        south, north = lev[0, low - 1 - k], lev[0, high + k]
        for n in levels:
            i, j = low - 1 - k + n, high + k - n
            south = lev[n, i] + coef[3, line(i), :] * south
            north = lev[n, j] + coef[4, line(j), :] * north
            lev[n, i] = south
            lev[n, j] = north
        return south, north

    def rim(d):
        for n in levels:
            for i in (low + WIND_STAGES + n - 1 - d, high - WIND_STAGES - n + d):
                advance(n, i)
                yield

    def chain(*parts):
        for part in parts:
            yield from part

    late(0)
    weave(rim(0))
    weave(react(couples[1:2]), chain(rim(1), rim(2)), 2)
    late(1)
    weave(react(couples[2 : 1 + WIND_STAGES]), ready(0))
    late(2)
    for k in range(depth - 1):
        values = arrive(k)
        pace = -(-2 * depth // (PARTS * CHEM_STEPS))
        weave(react([couples[1 + WIND_STAGES + k]], [values]), ready(k + 1), pace)
    mask_out[...] = mask_of(low, high - 1)
    done[0], done[rows - 1] = arrive(depth - 1)
    for side in range(2):
        wind_send(side).wait_send()
        for k in range(depth):
            halo_send(side, k).wait_send()


def finish(done, wind_new, weights, mask, tracers_out, winds_out, tail, out_sem, tail_sem, wind_sem):
    rows, species, width = done.shape
    block = species // PARTS
    copies = [pltpu.make_async_copy(wind_new, winds_out, wind_sem)]
    for r in range(1, rows - 1):
        copies.append(pltpu.make_async_copy(done.at[r], tracers_out.at[:, r, :], out_sem.at[r]))
    for copy in copies:
        copy.start()

    def store(part, values):
        own = slice(part * block, (part + 1) * block)
        tail[0, own] = values[:, :width]
        tail[1, own] = values[:, width:]
        if (part + 1) % (PARTS // PIECES) == 0:
            piece = (part + 1) // (PARTS // PIECES) - 1
            span = slice(piece * species // PIECES, (piece + 1) * species // PIECES)
            for end, r in ((0, 0), (1, rows - 1)):
                copy = pltpu.make_async_copy(
                    tail.at[end, span], tracers_out.at[span, r, :], tail_sem.at[end, piece]
                )
                copy.start()
                copies.append(copy)

    conc = jnp.concatenate([done[0], done[rows - 1]], axis=1)
    for _ in chemistry(weights, [conc], [mask[...]], store):
        pass
    for copy in copies:
        copy.wait()


def on_device(sizes, tracers, winds, linear, loss, left, right, active):
    species, rows, width = tracers.shape
    pairs = left.shape[0]
    held = rows + 2 * SUBS
    wrows = rows + 2 * (-(-(SUBS + WIND_STAGES) // 8) * 8)
    f32 = jnp.float32
    dma = pltpu.SemaphoreType.DMA
    anywhere = pl.BlockSpec(memory_space=pl.ANY)
    vmem = pl.BlockSpec(memory_space=pltpu.VMEM)
    lines = (1 + 2 * pairs) * species
    held_over = pl.pallas_call(
        functools.partial(kernel, sizes),
        out_shape=(
            pltpu.VMEM((rows, species, width), f32),
            pltpu.VMEM(winds.shape, f32),
            pltpu.VMEM((lines, 2 * species), jnp.bfloat16),
            pltpu.VMEM((1, 2 * width), f32),
        ),
        in_specs=[anywhere] * 7,
        out_specs=(vmem,) * 4,
        scratch_shapes=[
            pltpu.VMEM((SUBS + 1, held, species, width), f32),
            pltpu.VMEM((2, wrows, width), f32),
            pltpu.VMEM((5, wrows, width), f32),
            pltpu.VMEM(linear.shape, f32),
            pltpu.VMEM((1, species), f32),
            pltpu.VMEM((2,) + left.shape, f32),
            dma((rows,)),
            dma((4,)),
            dma,
            dma((2, SUBS)),
            dma((2, SUBS)),
            dma((2,)),
            dma((2,)),
            pltpu.SMEM(active.shape, active.dtype),
            dma,
            pltpu.SemaphoreType.REGULAR,
        ],
        compiler_params=pltpu.CompilerParams(collective_id=0, has_side_effects=True),
    )(active, tracers, winds, linear, loss.reshape(1, species), left, right)
    return pl.pallas_call(
        finish,
        out_shape=(
            jax.ShapeDtypeStruct(tracers.shape, f32),
            jax.ShapeDtypeStruct(winds.shape, f32),
        ),
        in_specs=[vmem] * 4,
        out_specs=(anywhere, anywhere),
        scratch_shapes=[pltpu.VMEM((2, species, width), f32), dma((rows,)), dma((2, PIECES)), dma],
    )(*(pltpu.with_memory_space_constraint(x, pltpu.VMEM) for x in held_over))


def solution(mesh):
    sizes = tuple(mesh.shape[axis] for axis in AXES)
    banded = P(None, AXES, None)
    return jax.shard_map(
        functools.partial(on_device, sizes),
        mesh=mesh,
        in_specs=(banded, banded, P(), P(), P(), P(), P(AXES)),
        out_specs=(banded, banded),
        check_vma=False,
    )
```

```python
import functools

import jax
import jax.numpy as jnp
from jax import lax
from jax.experimental import pallas as pl
from jax.experimental.pallas import tpu as pltpu
from jax.sharding import PartitionSpec as P

SUBS = 4
CHEM_STEPS = 3
WIND_STAGES = 3
PARTS = 2
PIECES = 2
FLOW = 6
LEAD = (2, 1)
EARLY = 2

DT_WIND = 0.1
VISCOSITY = 0.2
DT_TRACER = 0.1
DT_CHEM = 0.1

AXES = ("tile", "trac")
MESH = pl.DeviceIdType.MESH


def chemistry(weights, concs, masks, store=None):
    species = concs[0].shape[0]
    block = species // PARTS
    height = weights.shape[0] // PARTS
    pairs = (height // block - 1) // 2
    for step in range(CHEM_STEPS):
        for j, mask in enumerate(masks):
            conc = concs[j]
            high = conc.astype(jnp.bfloat16)
            low = (conc - high.astype(jnp.float32)).astype(jnp.bfloat16)
            high = jnp.concatenate([high, high], axis=0)
            low = jnp.concatenate([low, low], axis=0)
            blocks = []
            for part in range(PARTS):
                lhs = weights[part * height : (part + 1) * height]
                terms = jnp.dot(lhs, high, preferred_element_type=jnp.float32) + jnp.dot(
                    lhs, low, preferred_element_type=jnp.float32
                )
                rate = terms[:block]
                for p in range(pairs):
                    one = (1 + p) * block
                    two = (1 + pairs + p) * block
                    rate += terms[one : one + block] * terms[two : two + block]
                blocks.append(conc[part * block : (part + 1) * block] + rate * mask)
                if store is not None and step == CHEM_STEPS - 1:
                    store(part, blocks[-1])
                yield
            concs[j] = jnp.concatenate(blocks, axis=0)


def kernel(
    sizes,
    active,
    tracers,
    winds,
    linear,
    loss,
    left,
    right,
    done,
    wind_new,
    weights,
    mask_out,
    lev,
    wind,
    coef,
    lin_v,
    loss_v,
    fac_v,
    row_sem,
    par_sem,
    wind_sem,
    send_sem,
    recv_sem,
    wsend_sem,
    wrecv_sem,
    count_ref,
    count_sem,
    joined,
):
    tiles, tracs = sizes
    species, rows, width = tracers.shape
    pairs = left.shape[0]
    depth = SUBS
    reach = SUBS + WIND_STAGES
    wrows = wind.shape[1]
    base = (wrows - rows) // 2
    shift = base - depth
    devices = tiles * tracs
    me = lax.axis_index(AXES[0]) * tracs + lax.axis_index(AXES[1])
    up_flat = lax.rem(me + 1, devices)
    down_flat = lax.rem(me + devices - 1, devices)
    up = (up_flat // tracs, lax.rem(up_flat, tracs))
    down = (down_flat // tracs, lax.rem(down_flat, tracs))

    place = lax.axis_index(AXES[1])
    last = tracs - 1

    def tell(semaphore, neighbour):
        pl.semaphore_signal(semaphore, inc=1, device_id=neighbour, device_id_type=MESH)

    barrier = pltpu.get_barrier_semaphore()

    @pl.when(place < last)
    def _():
        tell(barrier, up)

    @pl.when(place < 2)
    def _():
        tell(barrier, down)


    order = []
    for k in range(depth):
        order += [rows - 1 - k, k]
    order += list(range(depth, rows - depth))

    def row_copy(r):
        return pltpu.make_async_copy(tracers.at[:, r, :], lev.at[0, depth + r], row_sem.at[r])

    own_wind = pltpu.make_async_copy(winds, wind.at[:, base : base + rows, :], wind_sem)
    own_wind.start()
    for r in order:
        row_copy(r).start()
    params = [
        pltpu.make_async_copy(linear, lin_v, par_sem.at[0]),
        pltpu.make_async_copy(loss, loss_v, par_sem.at[1]),
        pltpu.make_async_copy(left, fac_v.at[0], par_sem.at[2]),
        pltpu.make_async_copy(right, fac_v.at[1], par_sem.at[3]),
    ]
    for copy in params:
        copy.start()
    count_copy = pltpu.make_async_copy(active, count_ref, count_sem)
    count_copy.start()

    def wind_send(side):
        first = rows - reach if side == 0 else 0
        there = base - reach if side == 0 else base + rows
        return pltpu.make_async_remote_copy(
            src_ref=winds.at[:, first : first + reach, :],
            dst_ref=wind.at[:, there : there + reach, :],
            send_sem=wsend_sem.at[side],
            recv_sem=wrecv_sem.at[side],
            device_id=up if side == 0 else down,
            device_id_type=MESH,
        )

    def halo_send(side, k):
        here = rows - 1 - k if side == 0 else k
        there = depth - 1 - k if side == 0 else depth + rows + k
        return pltpu.make_async_remote_copy(
            src_ref=tracers.at[:, here, :],
            dst_ref=lev.at[0, there],
            send_sem=send_sem.at[side, k],
            recv_sem=recv_sem.at[side, k],
            device_id=up if side == 0 else down,
            device_id_type=MESH,
        )

    pl.semaphore_wait(barrier, jnp.where(place == last, 2, 1))

    @pl.when(place > 1)
    def _():
        tell(joined, down)

    @pl.when(place == last)
    def _():
        tell(joined, up)

    def send(side):
        wind_send(side).start()
        for k in range(depth):
            halo_send(side, k).start()

    def both(near, lead, early):
        turns = [(2 * k + 1, near, k) for k in range(early, depth)]
        turns += [(2 * (k - lead), 1 - near, k) for k in range(depth)]
        for _, side, k in sorted(turns):
            halo_send(side, k).start()

    @pl.when(place == 0)
    def _():
        wind_send(0).start()
        for k in range(EARLY):
            halo_send(0, k).start()

    @pl.when(jnp.logical_and(place > 0, place < last))
    def _():
        send(1)
        pl.semaphore_wait(joined, 1)
        send(0)

    @pl.when(place == last)
    def _():
        wind_send(0).start()
        wind_send(1).start()
        both(1, LEAD[1], 0)

    for copy in params:
        copy.wait()
    diag = lax.broadcasted_iota(jnp.int32, (species, species), 0) == lax.broadcasted_iota(
        jnp.int32, (species, species), 1
    )

    block = species // PARTS
    height = (1 + 2 * pairs) * block

    def put(slot, value):
        high = value.astype(jnp.bfloat16)
        low = (value - high.astype(jnp.float32)).astype(jnp.bfloat16)
        for part in range(PARTS):
            lines = pl.ds((part * (1 + 2 * pairs) + slot) * block, block)
            own = slice(part * block, (part + 1) * block)
            weights[lines, :species] = high[own]
            weights[lines, species : 2 * species] = low[own]

    put(0, DT_CHEM * (lin_v[...] - jnp.where(diag, loss_v[...], 0.0)))
    for p in range(pairs):
        put(1 + p, DT_CHEM * fac_v[0, p])
        put(1 + pairs + p, fac_v[1, p])

    for r in range(rows):
        row_copy(r).wait()
    own_wind.wait()

    def update_winds(first, end, keep_first, keep_end):
        raw = wind[:, first:end]
        u0, v0 = raw[0], raw[1]
        held = u0.shape[0]

        def tendency(u, v):
            def of(f):
                east = pltpu.roll(f, width - 1, 1)
                west = pltpu.roll(f, 1, 1)
                north = pltpu.roll(f, held - 1, 0)
                south = pltpu.roll(f, 1, 0)
                along = (east - west) * 0.5
                across = (north - south) * 0.5
                spread = east + west + north + south - 4.0 * f
                return -(u * along + v * across) + VISCOSITY * spread

            return of(u), of(v)

        tu, tv = tendency(u0, v0)
        u1, v1 = u0 + DT_WIND * tu, v0 + DT_WIND * tv
        tu, tv = tendency(u1, v1)
        u2 = 0.75 * u0 + 0.25 * (u1 + DT_WIND * tu)
        v2 = 0.75 * v0 + 0.25 * (v1 + DT_WIND * tv)
        tu, tv = tendency(u2, v2)
        u3 = u0 / 3.0 + 2.0 / 3.0 * (u2 + DT_WIND * tu)
        v3 = v0 / 3.0 + 2.0 / 3.0 * (v2 + DT_WIND * tv)
        lines = slice(keep_first, keep_end)
        own = slice(keep_first - first, keep_end - first)
        if held > rows:
            there = slice(max(keep_first, base) - base, min(keep_end, base + rows) - base)
            here = slice(there.start + base - first, there.stop + base - first)
            wind_new[0, there] = u3[here]
            wind_new[1, there] = v3[here]
        coef[0, lines] = (1.0 - DT_TRACER * (jnp.abs(u3) + jnp.abs(v3)))[own]
        coef[1, lines] = pltpu.roll(DT_TRACER * jnp.maximum(u3, 0.0), 1, 1)[own]
        coef[2, lines] = pltpu.roll(-DT_TRACER * jnp.minimum(u3, 0.0), width - 1, 1)[own]
        coef[3, lines] = pltpu.roll(DT_TRACER * jnp.maximum(v3, 0.0), 1, 0)[own]
        coef[4, lines] = pltpu.roll(-DT_TRACER * jnp.minimum(v3, 0.0), held - 1, 0)[own]

    def line(i):
        return pl.ds(i + shift, 1)

    def spread(level, i):
        q = lev[level - 1, i]
        moved = coef[0, line(i), :] * q
        moved += coef[1, line(i), :] * pltpu.roll(q, 1, 1)
        moved += coef[2, line(i), :] * pltpu.roll(q, width - 1, 1)
        return moved

    def advance(level, i):
        moved = spread(level, i)
        moved += coef[3, line(i), :] * lev[level - 1, i - 1]
        moved += coef[4, line(i), :] * lev[level - 1, i + 1]
        lev[level, i] = moved

    def sweep(spans):
        for level, first, last in spans:
            for i in range(first, last):
                advance(level, i)
                yield

    count_copy.wait()
    count = count_ref[0]
    lane = lax.broadcasted_iota(jnp.int32, (1, width), 1)

    def mask_of(*pair):
        cell = jnp.concatenate([(i - depth) * width + lane for i in pair], axis=1)
        return jnp.where(cell < count, 1.0, 0.0)

    def react(couples, values=None):
        concs, masks = [], []
        for n, (first, second) in enumerate(couples):
            pair = (lev[depth, first], lev[depth, second]) if values is None else values[n]
            concs.append(jnp.concatenate(pair, axis=1))
            masks.append(mask_of(first, second))
        yield from chemistry(weights, concs, masks)
        for (first, second), conc in zip(couples, concs):
            done[first - depth] = conc[:, :width]
            done[second - depth] = conc[:, width:]

    def weave(main, side=(), pace=1):
        side = iter(side)
        for _ in main:
            for _ in range(pace):
                next(side, None)
        for _ in side:
            pass

    update_winds(base, base + rows, base, base + rows)
    low, high = depth, depth + rows
    levels = range(1, depth + 1)
    inner = [(n, low + WIND_STAGES + n, high - WIND_STAGES - n) for n in levels]
    couples = [(low + depth + i, high - depth - 1 - i) for i in reversed(range(-depth, WIND_STAGES + 1))]
    assert 2 * WIND_STAGES + 2 == rows - 2 * depth and WIND_STAGES == 3
    weave(sweep(inner))

    def answer():
        pl.semaphore_wait(joined, 1)
        wind_send(1).start()
        both(0, LEAD[0], EARLY)

    first_tile = lax.axis_index(AXES[0]) == 0
    pl.when(jnp.logical_and(place == 0, jnp.logical_not(first_tile)))(answer)

    weave(react(couples[:1]))
    def ready(side, k):
        for n in levels:
            i, near = (high + k - n, -1) if side else (low - 1 - k + n, 1)
            lev[n, i] = spread(n, i) + coef[3 if side else 4, line(i), :] * lev[n - 1, i + near]
            yield

    def arrive(*sides_and_k):
        *sides, k = sides_and_k
        for side in sides:
            halo_send(side, k).wait_recv()
        ends = [lev[0, high + k if side else low - 1 - k] for side in sides]
        for n in levels:
            for at, side in enumerate(sides):
                i = high + k - n if side else low - 1 - k + n
                ends[at] = lev[n, i] + coef[4 if side else 3, line(i), :] * ends[at]
                lev[n, i] = ends[at]
        return ends

    def both_ready(k):
        return chain(ready(0, k), ready(1, k))

    def rim(side, d):
        for n in levels:
            advance(n, high - WIND_STAGES - n + d if side else low + WIND_STAGES + n - 1 - d)
            yield

    def chain(*parts):
        for part in parts:
            yield from part

    halfway = base + rows // 2
    pace = -(-2 * depth // (PARTS * CHEM_STEPS))

    def one_side(side):
        wind_send(side).wait_recv()
        if side:
            update_winds(base, wrows, halfway, wrows)
        else:
            update_winds(0, base + rows, 0, halfway)
        inner_rows = [couple[side] for couple in couples[1:3]]
        weave(chain(rim(side, 0), rim(side, 1)))
        weave(react([inner_rows]), rim(side, 2))

    def rest_inside():
        weave(react(couples[WIND_STAGES : 1 + WIND_STAGES]), both_ready(0))

    farthest = jnp.logical_and(place == 0, first_tile)

    @pl.when(place == last)
    def _():
        one_side(0)
        one_side(1)
        rest_inside()

    @pl.when(farthest)
    def _():
        one_side(1)
        answer()
        one_side(0)
        rest_inside()

    @pl.when(jnp.logical_and(place < last, jnp.logical_not(farthest)))
    def _():
        for side in range(2):
            wind_send(side).wait_recv()
        update_winds(0, wrows, 0, wrows)
        weave(chain(rim(0, 0), rim(1, 0)))
        weave(react(couples[1:2]), chain(*(rim(side, d) for d in (1, 2) for side in range(2))), 2)
        weave(react(couples[2 : 1 + WIND_STAGES]), both_ready(0))

    for k in range(depth - 1):
        values = arrive(0, 1, k)
        weave(react([couples[1 + WIND_STAGES + k]], [values]), both_ready(k + 1), pace)
    mask_out[...] = mask_of(low, high - 1)
    done[0], done[rows - 1] = arrive(0, 1, depth - 1)
    for side in range(2):
        wind_send(side).wait_send()
        for k in range(depth):
            halo_send(side, k).wait_send()


def finish(done, wind_new, weights, mask, tracers_out, winds_out, tail, out_sem, tail_sem, wind_sem):
    rows, species, width = done.shape
    block = species // PARTS
    copies = [pltpu.make_async_copy(wind_new, winds_out, wind_sem)]
    for r in range(1, rows - 1):
        copies.append(pltpu.make_async_copy(done.at[r], tracers_out.at[:, r, :], out_sem.at[r]))
    rest = iter(list(copies))

    def store(part, values):
        own = slice(part * block, (part + 1) * block)
        tail[0, own] = values[:, :width]
        tail[1, own] = values[:, width:]
        if (part + 1) % (PARTS // PIECES) == 0:
            piece = (part + 1) // (PARTS // PIECES) - 1
            span = slice(piece * species // PIECES, (piece + 1) * species // PIECES)
            for end, r in ((0, 0), (1, rows - 1)):
                copy = pltpu.make_async_copy(
                    tail.at[end, span], tracers_out.at[span, r, :], tail_sem.at[end, piece]
                )
                copy.start()
                copies.append(copy)

    conc = jnp.concatenate([done[0], done[rows - 1]], axis=1)
    for _ in chemistry(weights, [conc], [mask[...]], store):
        for copy in (next(rest, None) for _ in range(FLOW)):
            if copy is not None:
                copy.start()
    for copy in copies:
        copy.wait()


def on_device(sizes, tracers, winds, linear, loss, left, right, active):
    species, rows, width = tracers.shape
    pairs = left.shape[0]
    held = rows + 2 * SUBS
    wrows = rows + 2 * (-(-(SUBS + WIND_STAGES) // 8) * 8)
    f32 = jnp.float32
    dma = pltpu.SemaphoreType.DMA
    anywhere = pl.BlockSpec(memory_space=pl.ANY)
    vmem = pl.BlockSpec(memory_space=pltpu.VMEM)
    lines = (1 + 2 * pairs) * species
    held_over = pl.pallas_call(
        functools.partial(kernel, sizes),
        out_shape=(
            pltpu.VMEM((rows, species, width), f32),
            pltpu.VMEM(winds.shape, f32),
            pltpu.VMEM((lines, 2 * species), jnp.bfloat16),
            pltpu.VMEM((1, 2 * width), f32),
        ),
        in_specs=[anywhere] * 7,
        out_specs=(vmem,) * 4,
        scratch_shapes=[
            pltpu.VMEM((SUBS + 1, held, species, width), f32),
            pltpu.VMEM((2, wrows, width), f32),
            pltpu.VMEM((5, wrows, width), f32),
            pltpu.VMEM(linear.shape, f32),
            pltpu.VMEM((1, species), f32),
            pltpu.VMEM((2,) + left.shape, f32),
            dma((rows,)),
            dma((4,)),
            dma,
            dma((2, SUBS)),
            dma((2, SUBS)),
            dma((2,)),
            dma((2,)),
            pltpu.SMEM(active.shape, active.dtype),
            dma,
            pltpu.SemaphoreType.REGULAR,
        ],
        compiler_params=pltpu.CompilerParams(collective_id=0, has_side_effects=True),
    )(active, tracers, winds, linear, loss.reshape(1, species), left, right)
    return pl.pallas_call(
        finish,
        out_shape=(
            jax.ShapeDtypeStruct(tracers.shape, f32),
            jax.ShapeDtypeStruct(winds.shape, f32),
        ),
        in_specs=[vmem] * 4,
        out_specs=(anywhere, anywhere),
        scratch_shapes=[pltpu.VMEM((2, species, width), f32), dma((rows,)), dma((2, PIECES)), dma],
    )(*(pltpu.with_memory_space_constraint(x, pltpu.VMEM) for x in held_over))


def solution(mesh):
    sizes = tuple(mesh.shape[axis] for axis in AXES)
    banded = P(None, AXES, None)
    return jax.shard_map(
        functools.partial(on_device, sizes),
        mesh=mesh,
        in_specs=(banded, banded, P(), P(), P(), P(), P(AXES)),
        out_specs=(banded, banded),
        check_vma=False,
    )
```

```python
import functools

import jax
import jax.numpy as jnp
from jax import lax
from jax.experimental import pallas as pl
from jax.experimental.pallas import tpu as pltpu
from jax.sharding import PartitionSpec as P

SUBS = 4
CHEM_STEPS = 3
WIND_STAGES = 3
PARTS = 2
FLOW = 6
LEAD = (2, 1)
EARLY = 2

DT_WIND = 0.1
VISCOSITY = 0.2
DT_TRACER = 0.1
DT_CHEM = 0.1

AXES = ("tile", "trac")
MESH = pl.DeviceIdType.MESH


def chemistry(weights, concs, masks, store=None):
    species, width = concs[0].shape
    block = species // PARTS
    height = weights.shape[0] // PARTS
    pairs = (height // block - 1) // 2
    for step in range(CHEM_STEPS):
        for j, mask in enumerate(masks):
            conc = concs[j]
            high = conc.astype(jnp.bfloat16)
            low = (conc - high.astype(jnp.float32)).astype(jnp.bfloat16)
            parts = jnp.concatenate([high, low], axis=1)
            parts = jnp.concatenate([parts, parts], axis=0)
            blocks = []
            for part in range(PARTS):
                lhs = weights[part * height : (part + 1) * height]
                terms = jnp.dot(lhs, parts, preferred_element_type=jnp.float32)
                terms = terms[:, :width] + terms[:, width:]
                rate = terms[:block]
                for p in range(pairs):
                    one = (1 + p) * block
                    two = (1 + pairs + p) * block
                    rate += terms[one : one + block] * terms[two : two + block]
                blocks.append(conc[part * block : (part + 1) * block] + rate * mask)
                if store is not None and step == CHEM_STEPS - 1:
                    store(part, j, blocks[-1])
                yield
            concs[j] = jnp.concatenate(blocks, axis=0)


def kernel(
    sizes,
    active,
    tracers,
    winds,
    linear,
    loss,
    left,
    right,
    done,
    wind_new,
    weights,
    mask_out,
    lev,
    wind,
    coef,
    lin_v,
    loss_v,
    fac_v,
    row_sem,
    par_sem,
    wind_sem,
    send_sem,
    recv_sem,
    wsend_sem,
    wrecv_sem,
    count_ref,
    count_sem,
    joined,
):
    tiles, tracs = sizes
    species, rows, width = tracers.shape
    pairs = left.shape[0]
    depth = SUBS
    reach = SUBS + WIND_STAGES
    wrows = wind.shape[1]
    base = (wrows - rows) // 2
    shift = base - depth
    devices = tiles * tracs
    me = lax.axis_index(AXES[0]) * tracs + lax.axis_index(AXES[1])
    up_flat = lax.rem(me + 1, devices)
    down_flat = lax.rem(me + devices - 1, devices)
    up = (up_flat // tracs, lax.rem(up_flat, tracs))
    down = (down_flat // tracs, lax.rem(down_flat, tracs))

    place = lax.axis_index(AXES[1])
    last = tracs - 1

    def tell(semaphore, neighbour):
        pl.semaphore_signal(semaphore, inc=1, device_id=neighbour, device_id_type=MESH)

    barrier = pltpu.get_barrier_semaphore()

    @pl.when(place < last)
    def _():
        tell(barrier, up)

    @pl.when(place < 2)
    def _():
        tell(barrier, down)


    order = []
    for k in range(depth):
        order += [rows - 1 - k, k]
    order += list(range(depth, rows - depth))

    def row_copy(r):
        return pltpu.make_async_copy(tracers.at[:, r, :], lev.at[0, depth + r], row_sem.at[r])

    own_wind = pltpu.make_async_copy(winds, wind.at[:, base : base + rows, :], wind_sem)
    own_wind.start()
    for r in order:
        row_copy(r).start()
    params = [
        pltpu.make_async_copy(linear, lin_v, par_sem.at[0]),
        pltpu.make_async_copy(loss, loss_v, par_sem.at[1]),
        pltpu.make_async_copy(left, fac_v.at[0], par_sem.at[2]),
        pltpu.make_async_copy(right, fac_v.at[1], par_sem.at[3]),
    ]
    for copy in params:
        copy.start()
    count_copy = pltpu.make_async_copy(active, count_ref, count_sem)
    count_copy.start()

    def wind_send(side):
        first = rows - reach if side == 0 else 0
        there = base - reach if side == 0 else base + rows
        return pltpu.make_async_remote_copy(
            src_ref=winds.at[:, first : first + reach, :],
            dst_ref=wind.at[:, there : there + reach, :],
            send_sem=wsend_sem.at[side],
            recv_sem=wrecv_sem.at[side],
            device_id=up if side == 0 else down,
            device_id_type=MESH,
        )

    def halo_send(side, k):
        here = rows - 1 - k if side == 0 else k
        there = depth - 1 - k if side == 0 else depth + rows + k
        return pltpu.make_async_remote_copy(
            src_ref=tracers.at[:, here, :],
            dst_ref=lev.at[0, there],
            send_sem=send_sem.at[side, k],
            recv_sem=recv_sem.at[side, k],
            device_id=up if side == 0 else down,
            device_id_type=MESH,
        )

    pl.semaphore_wait(barrier, jnp.where(place == last, 2, 1))

    @pl.when(place > 1)
    def _():
        tell(joined, down)

    @pl.when(place == last)
    def _():
        tell(joined, up)

    def send(side):
        wind_send(side).start()
        for k in range(depth):
            halo_send(side, k).start()

    def both(near, lead, early):
        turns = [(2 * k + 1, near, k) for k in range(early, depth)]
        turns += [(2 * (k - lead), 1 - near, k) for k in range(depth)]
        for _, side, k in sorted(turns):
            halo_send(side, k).start()

    @pl.when(place == 0)
    def _():
        wind_send(0).start()
        for k in range(EARLY):
            halo_send(0, k).start()

    @pl.when(jnp.logical_and(place > 0, place < last))
    def _():
        send(1)
        pl.semaphore_wait(joined, 1)
        send(0)

    @pl.when(place == last)
    def _():
        wind_send(0).start()
        wind_send(1).start()
        both(1, LEAD[1], 0)

    for copy in params:
        copy.wait()
    diag = lax.broadcasted_iota(jnp.int32, (species, species), 0) == lax.broadcasted_iota(
        jnp.int32, (species, species), 1
    )

    block = species // PARTS
    height = (1 + 2 * pairs) * block

    def put(slot, value):
        high = value.astype(jnp.bfloat16)
        low = (value - high.astype(jnp.float32)).astype(jnp.bfloat16)
        for part in range(PARTS):
            lines = pl.ds((part * (1 + 2 * pairs) + slot) * block, block)
            own = slice(part * block, (part + 1) * block)
            weights[lines, :species] = high[own]
            weights[lines, species : 2 * species] = low[own]

    put(0, DT_CHEM * (lin_v[...] - jnp.where(diag, loss_v[...], 0.0)))
    for p in range(pairs):
        put(1 + p, DT_CHEM * fac_v[0, p])
        put(1 + pairs + p, fac_v[1, p])

    for r in range(rows):
        row_copy(r).wait()
    own_wind.wait()

    def update_winds(first, end, keep_first, keep_end):
        raw = wind[:, first:end]
        u0, v0 = raw[0], raw[1]
        held = u0.shape[0]

        def tendency(u, v):
            def of(f):
                east = pltpu.roll(f, width - 1, 1)
                west = pltpu.roll(f, 1, 1)
                north = pltpu.roll(f, held - 1, 0)
                south = pltpu.roll(f, 1, 0)
                along = (east - west) * 0.5
                across = (north - south) * 0.5
                spread = east + west + north + south - 4.0 * f
                return -(u * along + v * across) + VISCOSITY * spread

            return of(u), of(v)

        tu, tv = tendency(u0, v0)
        u1, v1 = u0 + DT_WIND * tu, v0 + DT_WIND * tv
        tu, tv = tendency(u1, v1)
        u2 = 0.75 * u0 + 0.25 * (u1 + DT_WIND * tu)
        v2 = 0.75 * v0 + 0.25 * (v1 + DT_WIND * tv)
        tu, tv = tendency(u2, v2)
        u3 = u0 / 3.0 + 2.0 / 3.0 * (u2 + DT_WIND * tu)
        v3 = v0 / 3.0 + 2.0 / 3.0 * (v2 + DT_WIND * tv)
        lines = slice(keep_first, keep_end)
        own = slice(keep_first - first, keep_end - first)
        if held > rows:
            there = slice(max(keep_first, base) - base, min(keep_end, base + rows) - base)
            here = slice(there.start + base - first, there.stop + base - first)
            wind_new[0, there] = u3[here]
            wind_new[1, there] = v3[here]
        coef[0, lines] = (1.0 - DT_TRACER * (jnp.abs(u3) + jnp.abs(v3)))[own]
        coef[1, lines] = pltpu.roll(DT_TRACER * jnp.maximum(u3, 0.0), 1, 1)[own]
        coef[2, lines] = pltpu.roll(-DT_TRACER * jnp.minimum(u3, 0.0), width - 1, 1)[own]
        coef[3, lines] = pltpu.roll(DT_TRACER * jnp.maximum(v3, 0.0), 1, 0)[own]
        coef[4, lines] = pltpu.roll(-DT_TRACER * jnp.minimum(v3, 0.0), held - 1, 0)[own]

    def line(i):
        return pl.ds(i + shift, 1)

    def spread(level, i):
        q = lev[level - 1, i]
        moved = coef[0, line(i), :] * q
        moved += coef[1, line(i), :] * pltpu.roll(q, 1, 1)
        moved += coef[2, line(i), :] * pltpu.roll(q, width - 1, 1)
        return moved

    def advance(level, i):
        moved = spread(level, i)
        moved += coef[3, line(i), :] * lev[level - 1, i - 1]
        moved += coef[4, line(i), :] * lev[level - 1, i + 1]
        lev[level, i] = moved

    def sweep(spans):
        for level, first, last in spans:
            for i in range(first, last):
                advance(level, i)
                yield

    count_copy.wait()
    count = count_ref[0]
    lane = lax.broadcasted_iota(jnp.int32, (1, width), 1)

    def mask_of(i):
        return jnp.where((i - depth) * width + lane < count, 1.0, 0.0)

    def react(couples, values=None):
        concs, masks = [], []
        for n, (first, second) in enumerate(couples):
            pair = (lev[depth, first], lev[depth, second]) if values is None else values[n]
            concs.extend(pair)
            masks.extend(mask_of(i) for i in (first, second))
        yield from chemistry(weights, concs, masks)
        for i, conc in zip((i for couple in couples for i in couple), concs):
            done[i - depth] = conc

    def weave(main, side=(), pace=1):
        side = iter(side)
        for _ in main:
            for _ in range(pace):
                next(side, None)
        for _ in side:
            pass

    update_winds(base, base + rows, base, base + rows)
    low, high = depth, depth + rows
    levels = range(1, depth + 1)
    inner = [(n, low + WIND_STAGES + n, high - WIND_STAGES - n) for n in levels]
    couples = [(low + depth + i, high - depth - 1 - i) for i in reversed(range(-depth, WIND_STAGES + 1))]
    assert 2 * WIND_STAGES + 2 == rows - 2 * depth and WIND_STAGES == 3
    weave(sweep(inner))

    def answer():
        pl.semaphore_wait(joined, 1)
        wind_send(1).start()
        both(0, LEAD[0], EARLY)

    first_tile = lax.axis_index(AXES[0]) == 0
    pl.when(jnp.logical_and(place == 0, jnp.logical_not(first_tile)))(answer)

    weave(react(couples[:1]))
    def ready(side, k):
        for n in levels:
            i, near = (high + k - n, -1) if side else (low - 1 - k + n, 1)
            lev[n, i] = spread(n, i) + coef[3 if side else 4, line(i), :] * lev[n - 1, i + near]
            yield

    def arrive(*sides_and_k):
        *sides, k = sides_and_k
        for side in sides:
            halo_send(side, k).wait_recv()
        ends = [lev[0, high + k if side else low - 1 - k] for side in sides]
        for n in levels:
            for at, side in enumerate(sides):
                i = high + k - n if side else low - 1 - k + n
                ends[at] = lev[n, i] + coef[4 if side else 3, line(i), :] * ends[at]
                lev[n, i] = ends[at]
        return ends

    def both_ready(k):
        return chain(ready(0, k), ready(1, k))

    def rim(side, d):
        for n in levels:
            advance(n, high - WIND_STAGES - n + d if side else low + WIND_STAGES + n - 1 - d)
            yield

    def chain(*parts):
        for part in parts:
            yield from part

    halfway = base + rows // 2
    pace = -(-2 * depth // (2 * PARTS * CHEM_STEPS))

    def one_side(side):
        wind_send(side).wait_recv()
        if side:
            update_winds(base, wrows, halfway, wrows)
        else:
            update_winds(0, base + rows, 0, halfway)
        inner_rows = [couple[side] for couple in couples[1:3]]
        weave(chain(rim(side, 0), rim(side, 1)))
        weave(react([inner_rows]), rim(side, 2))

    def rest_inside():
        weave(react(couples[WIND_STAGES : 1 + WIND_STAGES]), both_ready(0))

    farthest = jnp.logical_and(place == 0, first_tile)

    @pl.when(place == last)
    def _():
        one_side(0)
        one_side(1)
        rest_inside()

    @pl.when(farthest)
    def _():
        one_side(1)
        answer()
        one_side(0)
        rest_inside()

    @pl.when(jnp.logical_and(place < last, jnp.logical_not(farthest)))
    def _():
        for side in range(2):
            wind_send(side).wait_recv()
        update_winds(0, wrows, 0, wrows)
        weave(chain(rim(0, 0), rim(1, 0)))
        weave(react(couples[1:2]), chain(*(rim(side, d) for d in (1, 2) for side in range(2))), 2)
        weave(react(couples[2 : 1 + WIND_STAGES]), both_ready(0))

    for k in range(depth - 1):
        values = arrive(0, 1, k)
        weave(react([couples[1 + WIND_STAGES + k]], [values]), both_ready(k + 1), pace)
    mask_out[0], mask_out[1] = mask_of(low), mask_of(high - 1)
    done[0], done[rows - 1] = arrive(0, 1, depth - 1)
    for side in range(2):
        wind_send(side).wait_send()
        for k in range(depth):
            halo_send(side, k).wait_send()


def finish(done, wind_new, weights, mask, tracers_out, winds_out, tail, out_sem, tail_sem, wind_sem):
    rows, species, width = done.shape
    block = species // PARTS
    copies = [pltpu.make_async_copy(wind_new, winds_out, wind_sem)]
    for r in range(1, rows - 1):
        copies.append(pltpu.make_async_copy(done.at[r], tracers_out.at[:, r, :], out_sem.at[r]))
    rest = iter(list(copies))

    def store(part, end, values):
        own = slice(part * block, (part + 1) * block)
        tail[end, own] = values
        copy = pltpu.make_async_copy(
            tail.at[end, own], tracers_out.at[own, end * (rows - 1), :], tail_sem.at[end, part]
        )
        copy.start()
        copies.append(copy)

    ends = [done[0], done[rows - 1]]
    for _ in chemistry(weights, ends, [mask[0], mask[1]], store):
        for copy in (next(rest, None) for _ in range(FLOW)):
            if copy is not None:
                copy.start()
    for copy in copies:
        copy.wait()


def on_device(sizes, tracers, winds, linear, loss, left, right, active):
    species, rows, width = tracers.shape
    pairs = left.shape[0]
    held = rows + 2 * SUBS
    wrows = rows + 2 * (-(-(SUBS + WIND_STAGES) // 8) * 8)
    f32 = jnp.float32
    dma = pltpu.SemaphoreType.DMA
    anywhere = pl.BlockSpec(memory_space=pl.ANY)
    vmem = pl.BlockSpec(memory_space=pltpu.VMEM)
    lines = (1 + 2 * pairs) * species
    held_over = pl.pallas_call(
        functools.partial(kernel, sizes),
        out_shape=(
            pltpu.VMEM((rows, species, width), f32),
            pltpu.VMEM(winds.shape, f32),
            pltpu.VMEM((lines, 2 * species), jnp.bfloat16),
            pltpu.VMEM((2, 1, width), f32),
        ),
        in_specs=[anywhere] * 7,
        out_specs=(vmem,) * 4,
        scratch_shapes=[
            pltpu.VMEM((SUBS + 1, held, species, width), f32),
            pltpu.VMEM((2, wrows, width), f32),
            pltpu.VMEM((5, wrows, width), f32),
            pltpu.VMEM(linear.shape, f32),
            pltpu.VMEM((1, species), f32),
            pltpu.VMEM((2,) + left.shape, f32),
            dma((rows,)),
            dma((4,)),
            dma,
            dma((2, SUBS)),
            dma((2, SUBS)),
            dma((2,)),
            dma((2,)),
            pltpu.SMEM(active.shape, active.dtype),
            dma,
            pltpu.SemaphoreType.REGULAR,
        ],
        compiler_params=pltpu.CompilerParams(collective_id=0, has_side_effects=True),
    )(active, tracers, winds, linear, loss.reshape(1, species), left, right)
    return pl.pallas_call(
        finish,
        out_shape=(
            jax.ShapeDtypeStruct(tracers.shape, f32),
            jax.ShapeDtypeStruct(winds.shape, f32),
        ),
        in_specs=[vmem] * 4,
        out_specs=(anywhere, anywhere),
        scratch_shapes=[pltpu.VMEM((2, species, width), f32), dma((rows,)), dma((2, PARTS)), dma],
    )(*(pltpu.with_memory_space_constraint(x, pltpu.VMEM) for x in held_over))


def solution(mesh):
    sizes = tuple(mesh.shape[axis] for axis in AXES)
    banded = P(None, AXES, None)
    return jax.shard_map(
        functools.partial(on_device, sizes),
        mesh=mesh,
        in_specs=(banded, banded, P(), P(), P(), P(), P(AXES)),
        out_specs=(banded, banded),
        check_vma=False,
    )
```

```python
import functools

import jax
import jax.numpy as jnp
from jax import lax
from jax.experimental import pallas as pl
from jax.experimental.pallas import tpu as pltpu
from jax.sharding import PartitionSpec as P

SUBS = 4
CHEM_STEPS = 3
WIND_STAGES = 3
PARTS = 2
FLOW = 6
LEAD = (2, 1)
EARLY = 2

DT_WIND = 0.1
VISCOSITY = 0.2
DT_TRACER = 0.1
DT_CHEM = 0.1

AXES = ("tile", "trac")
MESH = pl.DeviceIdType.MESH


def chemistry(weights, concs, masks, store=None):
    species, width = concs[0].shape
    block = species // PARTS
    height = weights.shape[0] // PARTS
    pairs = (height // block - 1) // 2
    for step in range(CHEM_STEPS):
        for j, mask in enumerate(masks):
            conc = concs[j]
            high = conc.astype(jnp.bfloat16)
            low = (conc - high.astype(jnp.float32)).astype(jnp.bfloat16)
            parts = jnp.concatenate([high, low], axis=1)
            parts = jnp.concatenate([parts, parts], axis=0)
            blocks = []
            for part in range(PARTS):
                lhs = weights[part * height : (part + 1) * height]
                terms = jnp.dot(lhs, parts, preferred_element_type=jnp.float32)
                terms = terms[:, :width] + terms[:, width:]
                rate = terms[:block]
                for p in range(pairs):
                    one = (1 + p) * block
                    two = (1 + pairs + p) * block
                    rate += terms[one : one + block] * terms[two : two + block]
                blocks.append(conc[part * block : (part + 1) * block] + rate * mask)
                if store is not None and step == CHEM_STEPS - 1:
                    store(part, j, blocks[-1])
                yield
            concs[j] = jnp.concatenate(blocks, axis=0)


def kernel(
    sizes,
    active,
    tracers,
    winds,
    linear,
    loss,
    left,
    right,
    done,
    wind_new,
    weights,
    mask_out,
    lev,
    wind,
    coef,
    lin_v,
    loss_v,
    fac_v,
    row_sem,
    par_sem,
    wind_sem,
    send_sem,
    recv_sem,
    wsend_sem,
    wrecv_sem,
    count_ref,
    count_sem,
    joined,
):
    tiles, tracs = sizes
    species, rows, width = tracers.shape
    pairs = left.shape[0]
    depth = SUBS
    reach = SUBS + WIND_STAGES
    wrows = wind.shape[1]
    base = (wrows - rows) // 2
    shift = base - depth
    devices = tiles * tracs
    me = lax.axis_index(AXES[0]) * tracs + lax.axis_index(AXES[1])
    up_flat = lax.rem(me + 1, devices)
    down_flat = lax.rem(me + devices - 1, devices)
    up = (up_flat // tracs, lax.rem(up_flat, tracs))
    down = (down_flat // tracs, lax.rem(down_flat, tracs))

    place = lax.axis_index(AXES[1])
    last = tracs - 1

    def tell(semaphore, neighbour):
        pl.semaphore_signal(semaphore, inc=1, device_id=neighbour, device_id_type=MESH)

    barrier = pltpu.get_barrier_semaphore()

    @pl.when(place < last)
    def _():
        tell(barrier, up)

    @pl.when(place < 2)
    def _():
        tell(barrier, down)


    order = []
    for k in range(depth):
        order += [rows - 1 - k, k]
    order += list(range(depth, rows - depth))

    def row_copy(r):
        return pltpu.make_async_copy(tracers.at[:, r, :], lev.at[0, depth + r], row_sem.at[r])

    own_wind = pltpu.make_async_copy(winds, wind.at[:, base : base + rows, :], wind_sem)
    own_wind.start()
    for r in order:
        row_copy(r).start()
    params = [
        pltpu.make_async_copy(linear, lin_v, par_sem.at[0]),
        pltpu.make_async_copy(loss, loss_v, par_sem.at[1]),
        pltpu.make_async_copy(left, fac_v.at[0], par_sem.at[2]),
        pltpu.make_async_copy(right, fac_v.at[1], par_sem.at[3]),
    ]
    for copy in params:
        copy.start()
    count_copy = pltpu.make_async_copy(active, count_ref, count_sem)
    count_copy.start()

    def wind_send(side):
        first = rows - reach if side == 0 else 0
        there = base - reach if side == 0 else base + rows
        return pltpu.make_async_remote_copy(
            src_ref=winds.at[:, first : first + reach, :],
            dst_ref=wind.at[:, there : there + reach, :],
            send_sem=wsend_sem.at[side],
            recv_sem=wrecv_sem.at[side],
            device_id=up if side == 0 else down,
            device_id_type=MESH,
        )

    def halo_send(side, k):
        here = rows - 1 - k if side == 0 else k
        there = depth - 1 - k if side == 0 else depth + rows + k
        return pltpu.make_async_remote_copy(
            src_ref=tracers.at[:, here, :],
            dst_ref=lev.at[0, there],
            send_sem=send_sem.at[side, k],
            recv_sem=recv_sem.at[side, k],
            device_id=up if side == 0 else down,
            device_id_type=MESH,
        )

    pl.semaphore_wait(barrier, jnp.where(place == last, 2, 1))

    @pl.when(place > 1)
    def _():
        tell(joined, down)

    @pl.when(place == last)
    def _():
        tell(joined, up)

    def send(side):
        wind_send(side).start()
        for k in range(depth):
            halo_send(side, k).start()

    def both(near, lead, early):
        turns = [(2 * k + 1, near, k) for k in range(early, depth)]
        turns += [(2 * (k - lead), 1 - near, k) for k in range(depth)]
        for _, side, k in sorted(turns):
            halo_send(side, k).start()

    @pl.when(place == 0)
    def _():
        wind_send(0).start()
        for k in range(EARLY):
            halo_send(0, k).start()

    @pl.when(jnp.logical_and(place > 0, place < last))
    def _():
        wind_send(1).start()
        for k in range(2):
            halo_send(1, k).start()
        pl.semaphore_wait(joined, 1)
        wind_send(0).start()
        for k in range(depth):
            halo_send(0, k).start()
            if k + 2 < depth:
                halo_send(1, k + 2).start()

    @pl.when(place == last)
    def _():
        wind_send(0).start()
        wind_send(1).start()
        both(1, LEAD[1], 0)

    for copy in params:
        copy.wait()
    diag = lax.broadcasted_iota(jnp.int32, (species, species), 0) == lax.broadcasted_iota(
        jnp.int32, (species, species), 1
    )

    block = species // PARTS
    height = (1 + 2 * pairs) * block

    def put(slot, value):
        high = value.astype(jnp.bfloat16)
        low = (value - high.astype(jnp.float32)).astype(jnp.bfloat16)
        for part in range(PARTS):
            lines = pl.ds((part * (1 + 2 * pairs) + slot) * block, block)
            own = slice(part * block, (part + 1) * block)
            weights[lines, :species] = high[own]
            weights[lines, species : 2 * species] = low[own]

    put(0, DT_CHEM * (lin_v[...] - jnp.where(diag, loss_v[...], 0.0)))
    for p in range(pairs):
        put(1 + p, DT_CHEM * fac_v[0, p])
        put(1 + pairs + p, fac_v[1, p])

    for r in range(rows):
        row_copy(r).wait()
    own_wind.wait()

    def update_winds(first, end, keep_first, keep_end):
        raw = wind[:, first:end]
        u0, v0 = raw[0], raw[1]
        held = u0.shape[0]

        def tendency(u, v):
            def of(f):
                east = pltpu.roll(f, width - 1, 1)
                west = pltpu.roll(f, 1, 1)
                north = pltpu.roll(f, held - 1, 0)
                south = pltpu.roll(f, 1, 0)
                along = (east - west) * 0.5
                across = (north - south) * 0.5
                spread = east + west + north + south - 4.0 * f
                return -(u * along + v * across) + VISCOSITY * spread

            return of(u), of(v)

        tu, tv = tendency(u0, v0)
        u1, v1 = u0 + DT_WIND * tu, v0 + DT_WIND * tv
        tu, tv = tendency(u1, v1)
        u2 = 0.75 * u0 + 0.25 * (u1 + DT_WIND * tu)
        v2 = 0.75 * v0 + 0.25 * (v1 + DT_WIND * tv)
        tu, tv = tendency(u2, v2)
        u3 = u0 / 3.0 + 2.0 / 3.0 * (u2 + DT_WIND * tu)
        v3 = v0 / 3.0 + 2.0 / 3.0 * (v2 + DT_WIND * tv)
        lines = slice(keep_first, keep_end)
        own = slice(keep_first - first, keep_end - first)
        if held > rows:
            there = slice(max(keep_first, base) - base, min(keep_end, base + rows) - base)
            here = slice(there.start + base - first, there.stop + base - first)
            wind_new[0, there] = u3[here]
            wind_new[1, there] = v3[here]
        coef[0, lines] = (1.0 - DT_TRACER * (jnp.abs(u3) + jnp.abs(v3)))[own]
        coef[1, lines] = pltpu.roll(DT_TRACER * jnp.maximum(u3, 0.0), 1, 1)[own]
        coef[2, lines] = pltpu.roll(-DT_TRACER * jnp.minimum(u3, 0.0), width - 1, 1)[own]
        coef[3, lines] = pltpu.roll(DT_TRACER * jnp.maximum(v3, 0.0), 1, 0)[own]
        coef[4, lines] = pltpu.roll(-DT_TRACER * jnp.minimum(v3, 0.0), held - 1, 0)[own]

    def line(i):
        return pl.ds(i + shift, 1)

    def spread(level, i):
        q = lev[level - 1, i]
        moved = coef[0, line(i), :] * q
        moved += coef[1, line(i), :] * pltpu.roll(q, 1, 1)
        moved += coef[2, line(i), :] * pltpu.roll(q, width - 1, 1)
        return moved

    def advance(level, i):
        moved = spread(level, i)
        moved += coef[3, line(i), :] * lev[level - 1, i - 1]
        moved += coef[4, line(i), :] * lev[level - 1, i + 1]
        lev[level, i] = moved

    def sweep(spans):
        for level, first, last in spans:
            for i in range(first, last):
                advance(level, i)
                yield

    count_copy.wait()
    count = count_ref[0]
    lane = lax.broadcasted_iota(jnp.int32, (1, width), 1)

    def mask_of(i):
        return jnp.where((i - depth) * width + lane < count, 1.0, 0.0)

    def react(couples, values=None):
        concs, masks = [], []
        for n, (first, second) in enumerate(couples):
            pair = (lev[depth, first], lev[depth, second]) if values is None else values[n]
            concs.extend(pair)
            masks.extend(mask_of(i) for i in (first, second))
        yield from chemistry(weights, concs, masks)
        for i, conc in zip((i for couple in couples for i in couple), concs):
            done[i - depth] = conc

    def weave(main, side=(), pace=1):
        side = iter(side)
        for _ in main:
            for _ in range(pace):
                next(side, None)
        for _ in side:
            pass

    update_winds(base, base + rows, base, base + rows)
    low, high = depth, depth + rows
    levels = range(1, depth + 1)
    inner = [(n, low + WIND_STAGES + n, high - WIND_STAGES - n) for n in levels]
    couples = [(low + depth + i, high - depth - 1 - i) for i in reversed(range(-depth, WIND_STAGES + 1))]
    assert 2 * WIND_STAGES + 2 == rows - 2 * depth and WIND_STAGES == 3
    weave(sweep(inner))

    def answer():
        pl.semaphore_wait(joined, 1)
        wind_send(1).start()
        both(0, LEAD[0], EARLY)

    first_tile = lax.axis_index(AXES[0]) == 0
    pl.when(jnp.logical_and(place == 0, jnp.logical_not(first_tile)))(answer)

    weave(react(couples[:1]))
    def ready(side, k):
        for n in levels:
            i, near = (high + k - n, -1) if side else (low - 1 - k + n, 1)
            lev[n, i] = spread(n, i) + coef[3 if side else 4, line(i), :] * lev[n - 1, i + near]
            yield

    def arrive(*sides_and_k):
        *sides, k = sides_and_k
        for side in sides:
            halo_send(side, k).wait_recv()
        ends = [lev[0, high + k if side else low - 1 - k] for side in sides]
        for n in levels:
            for at, side in enumerate(sides):
                i = high + k - n if side else low - 1 - k + n
                ends[at] = lev[n, i] + coef[4 if side else 3, line(i), :] * ends[at]
                lev[n, i] = ends[at]
        return ends

    def both_ready(k):
        return chain(ready(0, k), ready(1, k))

    def rim(side, d):
        for n in levels:
            advance(n, high - WIND_STAGES - n + d if side else low + WIND_STAGES + n - 1 - d)
            yield

    def chain(*parts):
        for part in parts:
            yield from part

    halfway = base + rows // 2
    pace = -(-2 * depth // (2 * PARTS * CHEM_STEPS))

    def one_side(side):
        wind_send(side).wait_recv()
        if side:
            update_winds(base, wrows, halfway, wrows)
        else:
            update_winds(0, base + rows, 0, halfway)
        inner_rows = [couple[side] for couple in couples[1:3]]
        weave(chain(rim(side, 0), rim(side, 1)))
        weave(react([inner_rows]), rim(side, 2))

    def rest_inside():
        weave(react(couples[WIND_STAGES : 1 + WIND_STAGES]), both_ready(0))

    farthest = jnp.logical_and(place == 0, first_tile)

    @pl.when(place == last)
    def _():
        one_side(0)
        one_side(1)
        rest_inside()

    @pl.when(farthest)
    def _():
        one_side(1)
        answer()
        one_side(0)
        rest_inside()

    @pl.when(jnp.logical_and(place < last, jnp.logical_not(farthest)))
    def _():
        for side in range(2):
            wind_send(side).wait_recv()
        update_winds(0, wrows, 0, wrows)
        weave(chain(rim(0, 0), rim(1, 0)))
        weave(react(couples[1:2]), chain(*(rim(side, d) for d in (1, 2) for side in range(2))), 2)
        weave(react(couples[2 : 1 + WIND_STAGES]), both_ready(0))

    for k in range(depth - 1):
        values = arrive(0, 1, k)
        weave(react([couples[1 + WIND_STAGES + k]], [values]), both_ready(k + 1), pace)
    mask_out[0], mask_out[1] = mask_of(low), mask_of(high - 1)
    done[0], done[rows - 1] = arrive(0, 1, depth - 1)
    for side in range(2):
        wind_send(side).wait_send()
        for k in range(depth):
            halo_send(side, k).wait_send()


def finish(done, wind_new, weights, mask, tracers_out, winds_out, tail, out_sem, tail_sem, wind_sem):
    rows, species, width = done.shape
    block = species // PARTS
    copies = [pltpu.make_async_copy(wind_new, winds_out, wind_sem)]
    for r in range(1, rows - 1):
        copies.append(pltpu.make_async_copy(done.at[r], tracers_out.at[:, r, :], out_sem.at[r]))
    rest = iter(list(copies))

    def store(part, end, values):
        own = slice(part * block, (part + 1) * block)
        tail[end, own] = values
        copy = pltpu.make_async_copy(
            tail.at[end, own], tracers_out.at[own, end * (rows - 1), :], tail_sem.at[end, part]
        )
        copy.start()
        copies.append(copy)

    ends = [done[0], done[rows - 1]]
    for _ in chemistry(weights, ends, [mask[0], mask[1]], store):
        for copy in (next(rest, None) for _ in range(FLOW)):
            if copy is not None:
                copy.start()
    for copy in copies:
        copy.wait()


def on_device(sizes, tracers, winds, linear, loss, left, right, active):
    species, rows, width = tracers.shape
    pairs = left.shape[0]
    held = rows + 2 * SUBS
    wrows = rows + 2 * (-(-(SUBS + WIND_STAGES) // 8) * 8)
    f32 = jnp.float32
    dma = pltpu.SemaphoreType.DMA
    anywhere = pl.BlockSpec(memory_space=pl.ANY)
    vmem = pl.BlockSpec(memory_space=pltpu.VMEM)
    lines = (1 + 2 * pairs) * species
    held_over = pl.pallas_call(
        functools.partial(kernel, sizes),
        out_shape=(
            pltpu.VMEM((rows, species, width), f32),
            pltpu.VMEM(winds.shape, f32),
            pltpu.VMEM((lines, 2 * species), jnp.bfloat16),
            pltpu.VMEM((2, 1, width), f32),
        ),
        in_specs=[anywhere] * 7,
        out_specs=(vmem,) * 4,
        scratch_shapes=[
            pltpu.VMEM((SUBS + 1, held, species, width), f32),
            pltpu.VMEM((2, wrows, width), f32),
            pltpu.VMEM((5, wrows, width), f32),
            pltpu.VMEM(linear.shape, f32),
            pltpu.VMEM((1, species), f32),
            pltpu.VMEM((2,) + left.shape, f32),
            dma((rows,)),
            dma((4,)),
            dma,
            dma((2, SUBS)),
            dma((2, SUBS)),
            dma((2,)),
            dma((2,)),
            pltpu.SMEM(active.shape, active.dtype),
            dma,
            pltpu.SemaphoreType.REGULAR,
        ],
        compiler_params=pltpu.CompilerParams(collective_id=0, has_side_effects=True),
    )(active, tracers, winds, linear, loss.reshape(1, species), left, right)
    return pl.pallas_call(
        finish,
        out_shape=(
            jax.ShapeDtypeStruct(tracers.shape, f32),
            jax.ShapeDtypeStruct(winds.shape, f32),
        ),
        in_specs=[vmem] * 4,
        out_specs=(anywhere, anywhere),
        scratch_shapes=[pltpu.VMEM((2, species, width), f32), dma((rows,)), dma((2, PARTS)), dma],
    )(*(pltpu.with_memory_space_constraint(x, pltpu.VMEM) for x in held_over))


def solution(mesh):
    sizes = tuple(mesh.shape[axis] for axis in AXES)
    banded = P(None, AXES, None)
    return jax.shard_map(
        functools.partial(on_device, sizes),
        mesh=mesh,
        in_specs=(banded, banded, P(), P(), P(), P(), P(AXES)),
        out_specs=(banded, banded),
        check_vma=False,
    )
```
